128 devices in a mesh: mem: 8 (over z, core), lat: 16 (over y, x).
Axes of the slice: x: 4, y: 4, z: 4, core: 2. Of those that a mesh axis runs over, the one named last changes fastest.
Arguments:
- perturbations: bfloat16 [256, 3, 384, 1280], P('mem', None, 'lat'), may hold values from -0.375 to 0.375
- control: float32 [256, 96, 320], P('mem', 'lat'), may hold values from -6 to 6
- innovations: float32 [3, 384, 1280], P(None, 'lat'), may hold values from -6 to 6
- thresholds: float32 [3], replicated, may hold values from 0.4 to 1.5
Outputs:
- weights: float32 [256, 96, 320], P('mem', 'lat')
- increment: float32 [3, 384, 1280], P(None, 'lat', 'mem')
The draws below stay inside these ranges and needn't reach their ends.
All inputs are finite; a program needn't handle non-finite values.
Results may differ from the reference program's by a relative error of at most 0.0003.
Values sent between devices are 32-bit elements; how exact they have to be, the bound alone decides.
A program may use at most 64 MiB of HBM per device.

```python
import math
import jax
import jax.numpy as jnp
from jax import lax

MEM_DEV = 32
CLON = 320
VARS = 3
RATIO = 4
HALF = 5
STEPS = 2
MEMBERS = 256
NCR = 96
FROWS = 384
FLON = 1280
N_MEM = 8


def block_scale(rng, extent, cuts, smallest, largest):
    def one(position, shards_of):
        draws = jax.random.uniform(jax.random.fold_in(jax.random.fold_in(rng, 6), position), (shards_of,), jnp.float32, smallest / len(cuts), largest / len(cuts))
        return jnp.repeat(jnp.exp(draws), extent[position] // shards_of).reshape((-1,) + (1,) * (len(extent) - position - 1))

    loudness = one(*cuts[0])
    for cut in cuts[1:]:
        loudness = loudness * one(*cut)
    return loudness


def noise(stream_key, shape, spread, bound, pieces=(), kind=jnp.bfloat16):
    values = jax.random.normal(stream_key, shape, jnp.float32) * spread
    if len(pieces) > 0:
        values = block_scale(stream_key, shape, pieces, -0.22, 0.18) * values
    return jnp.clip(values, min=-bound, max=bound).astype(kind)


def setup_inputs(seed: int = 0) -> dict:
    keys = jax.random.split(jax.random.key(seed), 5)
    return {
        "perturbations": noise(keys[0], (MEMBERS, VARS, FROWS, FLON), MEMBERS ** -0.5, 0.375, ((0, 8), (2, 16))),
        "control": noise(keys[1], (MEMBERS, NCR, CLON), 1.0, 6.0, ((0, 8), (1, 16)), jnp.float32),
        "innovations": noise(keys[2], (VARS, FROWS, FLON), 1.0, 6.0, ((1, 16),), jnp.float32),
        "thresholds": jnp.clip(jnp.exp(jax.random.uniform(keys[3], (VARS,), jnp.float32, math.log(0.4), math.log(1.5))), 0.4, 1.5),
    }


def tent_table(fine_count, coarse_count, periodic):
    fine_pos = jnp.arange(fine_count, dtype=jnp.float32)[:, None]
    coarse_pos = jnp.arange(coarse_count, dtype=jnp.float32)[None, :]
    distance = fine_pos + 0.5 - RATIO * coarse_pos - RATIO / 2
    if periodic:
        distance = jnp.mod(distance + fine_count / 2, fine_count) - fine_count / 2
    return jnp.maximum(0.0, 1.0 - jnp.abs(distance) / RATIO)


def smooth_table(count):
    distance = jnp.abs(jnp.arange(count, dtype=jnp.float32)[None, :] - jnp.arange(count, dtype=jnp.float32)[:, None])
    return jnp.where(distance <= HALF, (1.0 - distance / (HALF + 1)) / 2, 0.0)


def reference(perturbations, control, innovations, thresholds):
    highest = lax.Precision.HIGHEST
    smooth = smooth_table(NCR)
    lat_up = tent_table(FROWS, NCR, False)
    lon_up = tent_table(FLON, CLON, True).T
    pert_blocks = perturbations.reshape(N_MEM, MEM_DEV, VARS, FROWS, FLON)

    def forward(weights):
        def add_block(running, blocks):
            pert, group = blocks
            smoothed = jnp.einsum("jq,bqc->bjc", smooth, group, precision=highest)
            rowwise = jnp.einsum("iq,bqc->bic", lat_up, smoothed, precision=highest)
            refined = jnp.einsum("bic,cf->bif", rowwise, lon_up, precision=highest)
            return running + jnp.sum(pert.astype(jnp.float32) * refined[:, None], axis=0), None
        start = jnp.zeros((VARS, FROWS, FLON), jnp.float32)
        result, unused = lax.scan(add_block, start, (pert_blocks, weights.reshape(N_MEM, MEM_DEV, NCR, CLON)))
        return result

    def adjoint(misfit, weights):
        def one_block(blocks):
            pert, group = blocks
            weighted = jnp.sum(pert.astype(jnp.float32) * misfit[None], axis=1)
            columns = jnp.einsum("bif,cf->bic", weighted, lon_up, precision=highest)
            coarse = jnp.einsum("iq,bic->bqc", lat_up, columns, precision=highest)
            return group + jnp.einsum("jq,bqc->bjc", smooth, coarse, precision=highest)
        result = lax.map(one_block, (pert_blocks, weights.reshape(N_MEM, MEM_DEV, NCR, CLON)))
        return result.reshape(MEMBERS, NCR, CLON)

    weights = control
    increment = forward(control)
    for iteration in range(STEPS):
        limit = thresholds[:, None, None]
        misfit = jnp.clip(increment - innovations, -limit, limit)
        gradient = adjoint(misfit, weights)
        image = forward(gradient)
        grad_sq = jnp.sum(gradient * gradient)
        image_sq = jnp.sum(image * image)
        step_len = grad_sq / (grad_sq + image_sq)
        weights = weights - step_len * gradient
        increment = increment - step_len * image
    return weights, increment
```

```python
import functools

import jax
import jax.numpy as jnp
import numpy as np
from jax import lax
from jax.experimental import pallas as pl
from jax.experimental.pallas import tpu as pltpu
from jax.sharding import PartitionSpec as P

RATIO = 4
HALF = 5
STEPS = 2
GROUP = 8
LANES = 128
MESH = pl.DeviceIdType.MESH
SCALE = 96.0


def tent(distance):
    return np.maximum(0.0, 1.0 - np.abs(distance) / RATIO)


def row_operator(coarse_rows, first, last):
    fine = np.arange(RATIO * coarse_rows)[:, None]
    inner = np.arange(-1, coarse_rows + 1)
    up = tent(fine + 0.5 - RATIO * inner[None, :] - RATIO / 2)
    if first:
        up[:, 0] = 0.0
    if last:
        up[:, -1] = 0.0
    outer = np.arange(-coarse_rows, 2 * coarse_rows)
    gap = np.abs(inner[:, None] - outer[None, :])
    smooth = np.where(gap <= HALF, (1.0 - gap / (HALF + 1)) / 2, 0.0)
    return np.rint(SCALE * up @ smooth)


def block_rows(operator):
    fine, wide = operator.shape
    out = np.zeros((GROUP, fine, wide, GROUP))
    for member in range(GROUP):
        out[member, :, :, member] = operator
    return out.reshape(GROUP * fine, wide * GROUP)


def tables(coarse_rows):
    ops = [block_rows(row_operator(coarse_rows, *ends)) for ends in ((True, False), (False, False), (False, True))]
    rows_up = np.stack(ops)
    rows_down = np.stack([op.T for op in ops])
    fine = np.arange(2 * LANES)[None, :]
    narrow = tent(LANES + fine + 0.5 - RATIO * np.arange(LANES)[:, None] - RATIO / 2)
    wide = tent(3 * LANES + fine + 0.5 - RATIO * np.arange(2 * LANES)[:, None] - RATIO / 2)
    narrow_up = np.concatenate([narrow, narrow], 0)
    narrow_down = np.concatenate([narrow.T, narrow.T], 0)
    wide_down = np.concatenate([wide.T, wide.T], 0)
    return [jnp.asarray(t, jnp.bfloat16) for t in (rows_up, rows_down, narrow_up, wide, narrow_down, wide_down)]


def split(x):
    high = x.astype(jnp.bfloat16)
    return high, (x - high.astype(jnp.float32)).astype(jnp.bfloat16)


def dot(a, b):
    return jnp.dot(a, b, preferred_element_type=jnp.float32)


def kernel(
    n_mem, n_lat, seg,
    pert_hbm, control, innov, thr, rows_up, rows_down, narrow_up, wide_up, narrow_down, wide_down,
    weights_out, inc_out,
    pert, halo, part_send, part_recv, own, w, acc, gather, inc, misfit, obs, rs_recv,
    sc_lat_send, sc_lat, sc_mem_send, sc_mem,
    pert_sem, g_send, g_recv, c_send, c_recv, rs_ss, rs_rs, ag_ss, ag_rs, sl_ss, sl_rs, sm_ss, sm_rs,
):
    mem = lax.axis_index("mem")
    lat = lax.axis_index("lat")
    chunks = pert.shape[0] // GROUP
    n_vars = pert.shape[1]
    fine = pert.shape[2]
    tiles = pert.shape[3] // LANES
    tile_rows = n_vars * fine
    part = gather.shape[0] // n_mem
    half = seg // 2
    case = jnp.where(lat == 0, 0, jnp.where(lat == n_lat - 1, 2, 1))
    up_id = (mem, jnp.maximum(lat - 1, 0))
    down_id = (mem, jnp.minimum(lat + 1, n_lat - 1))
    has_up = lat > 0
    has_down = lat < n_lat - 1

    def pert_copy(c):
        rows = pl.ds(c * GROUP, GROUP)
        return pltpu.make_async_copy(pert_hbm.at[rows], pert.at[rows], pert_sem.at[c])

    for c in range(chunks):
        pert_copy(c).start()

    barrier = pltpu.get_barrier_semaphore()
    for k in range(1, n_mem):
        pl.semaphore_signal(barrier, inc=1, device_id=(lax.rem(mem + k, n_mem), lat), device_id_type=MESH)
    for k in range(1, n_lat):
        pl.semaphore_signal(barrier, inc=1, device_id=(mem, lax.rem(lat + k, n_lat)), device_id_type=MESH)
    pl.semaphore_wait(barrier, n_mem + n_lat - 2)

    def g_copy(c, up):
        return pltpu.make_async_remote_copy(
            src_ref=halo.at[1, c], dst_ref=halo.at[2 if up else 0, c],
            send_sem=g_send.at[0 if up else 1, c], recv_sem=g_recv.at[0 if up else 1, c],
            device_id=up_id if up else down_id, device_id_type=MESH)

    def c_copy(c, up):
        return pltpu.make_async_remote_copy(
            src_ref=part_send.at[0 if up else 1, c], dst_ref=part_recv.at[0 if up else 1, c],
            send_sem=c_send.at[0 if up else 1, c], recv_sem=c_recv.at[0 if up else 1, c],
            device_id=up_id if up else down_id, device_id_type=MESH)

    def send_both(copy, c):
        @pl.when(has_up)
        def _():
            copy(c, True).start()

        @pl.when(has_down)
        def _():
            copy(c, False).start()

    def recv_both(copy, c):
        @pl.when(has_down)
        def _():
            copy(c, True).wait_recv()

        @pl.when(has_up)
        def _():
            copy(c, False).wait_recv()

    def sent_both(copy, c):
        @pl.when(has_up)
        def _():
            copy(c, True).wait_send()

        @pl.when(has_down)
        def _():
            copy(c, False).wait_send()

    lane = lax.broadcasted_iota(jnp.int32, (half, LANES), 1)
    left = lane < LANES // 2

    def swap(x):
        return pltpu.roll(x, LANES // 2, 1)

    def pack(x, factor):
        e0, e1, e2 = x[:, :LANES], x[:, LANES:2 * LANES], x[:, 2 * LANES:]
        a, b = e2[:half], e2[half:]
        sa, sb = swap(a), swap(b)
        top = e0[:half] + jnp.where(left, sa, 0.0)
        bottom = e0[half:] + jnp.where(left, sb, 0.0)
        tail = jnp.where(left, a, sb)
        return jnp.concatenate([top, bottom, e1, tail], axis=0) * factor

    def unpack(x):
        e0, e1, tail = x[:seg], x[seg:2 * seg], x[2 * seg:]
        st = swap(tail)
        a = jnp.where(left, tail, swap(e0[:half]))
        b = jnp.where(left, st, swap(e0[half:]))
        return jnp.concatenate([e0, e1, jnp.concatenate([a, b], axis=0)], axis=1)

    def lane_pair(j):
        return 2 * j + 1, (2 * j + 2) % tiles

    def forward_chunk(c):
        block = jnp.concatenate([unpack(halo[s, c]) for s in range(3)], axis=0)
        high, low = split(block)
        table = rows_up[case]
        rows = dot(table, high) + dot(table, low)
        high, low = split(rows)
        members = pl.ds(c * GROUP, GROUP)
        for j in range(tiles // 2):
            g = j // 2
            cols = slice(g * LANES, (g + 1) * LANES)
            if j % 2 == 0:
                fine_rows = dot(jnp.concatenate([high[:, cols], low[:, cols]], axis=1), narrow_up[...])
            else:
                cols = slice(g * LANES, (g + 2) * LANES)
                fine_rows = dot(high[:, cols], wide_up[...]) + dot(low[:, cols], wide_up[...])
            for h, t in enumerate(lane_pair(j)):
                field = fine_rows[:, h * LANES:(h + 1) * LANES].reshape(GROUP, fine, LANES)
                for v in range(n_vars):
                    p = pert[members, v, :, t * LANES:(t + 1) * LANES].astype(jnp.float32)
                    where = pl.ds(t * tile_rows + v * fine, fine)
                    acc[where, :] += jnp.sum(p * field, axis=0)

    def adjoint_chunk(c):
        members = pl.ds(c * GROUP, GROUP)
        sums = [None] * 3

        def add(i, value):
            sums[i] = value if sums[i] is None else sums[i] + value

        for j in range(tiles // 2):
            pieces = []
            for t in lane_pair(j):
                total = None
                for v in range(n_vars):
                    p = pert[members, v, :, t * LANES:(t + 1) * LANES].astype(jnp.float32)
                    term = p * misfit[pl.ds(t * tile_rows + v * fine, fine), :][None]
                    total = term if total is None else total + term
                pieces.append(split(total.reshape(GROUP * fine, LANES)))
            lhs = jnp.concatenate([pieces[0][0], pieces[1][0], pieces[0][1], pieces[1][1]], axis=1)
            g = j // 2
            if j % 2 == 0:
                add(g, dot(lhs, narrow_down[...]))
            else:
                both = dot(lhs, wide_down[...])
                add(g, both[:, :LANES])
                add(g + 1, both[:, LANES:])
        high, low = split(jnp.concatenate(sums, axis=1))
        table = rows_down[case]
        coarse = dot(table, high) + dot(table, low)
        part_send[0, c] = pack(coarse[:seg], 1.0 / SCALE)
        own[c] = pack(coarse[seg:2 * seg], 1.0 / SCALE)
        part_send[1, c] = pack(coarse[2 * seg:], 1.0 / SCALE)

    def forward_all():
        acc[...] = jnp.zeros_like(acc)

        def body(c, carry):
            recv_both(g_copy, c)
            forward_chunk(c)
            return carry

        lax.fori_loop(0, chunks, body, 0)

        def body_sent(c, carry):
            sent_both(g_copy, c)
            return carry

        lax.fori_loop(0, chunks, body_sent, 0)

    def part_rows(k):
        return pl.ds(pl.multiple_of(k * part, 8), part)

    def rs_copy(k):
        peer = lax.rem(mem + k, n_mem)
        return pltpu.make_async_remote_copy(
            src_ref=acc.at[part_rows(peer)], dst_ref=rs_recv.at[k - 1],
            send_sem=rs_ss.at[k - 1], recv_sem=rs_rs.at[k - 1], device_id=(peer, lat), device_id_type=MESH)

    def ag_copy(k):
        peer = lax.rem(mem + k, n_mem)
        return pltpu.make_async_remote_copy(
            src_ref=gather.at[part_rows(mem)], dst_ref=gather.at[part_rows(mem)],
            send_sem=ag_ss.at[k - 1], recv_sem=ag_rs.at[k - 1], device_id=(peer, lat), device_id_type=MESH)

    def reduce_scatter():
        for k in range(1, n_mem):
            rs_copy(k).start()
        for k in range(1, n_mem):
            rs_copy(k).wait_recv()
        total = acc[part_rows(mem), :]
        for k in range(1, n_mem):
            total = total + rs_recv[k - 1]
        total = total * (1.0 / SCALE)
        gather[part_rows(mem), :] = total
        for k in range(1, n_mem):
            rs_copy(k).wait_send()
        return total

    def gather_start():
        for k in range(1, n_mem):
            ag_copy(k).start()

    def gather_wait():
        for k in range(1, n_mem):
            ag_copy(k).wait_recv()
        for k in range(1, n_mem):
            ag_copy(k).wait_send()

    def sl_copy(it, k):
        return pltpu.make_async_remote_copy(
            src_ref=sc_lat_send, dst_ref=sc_lat.at[it, k - 1],
            send_sem=sl_ss.at[it, k - 1], recv_sem=sl_rs.at[it, k - 1],
            device_id=(mem, lax.rem(lat + k, n_lat)), device_id_type=MESH)

    def sm_copy(it, k):
        return pltpu.make_async_remote_copy(
            src_ref=sc_mem_send, dst_ref=sc_mem.at[it, k - 1],
            send_sem=sm_ss.at[it, k - 1], recv_sem=sm_rs.at[it, k - 1],
            device_id=(lax.rem(mem + k, n_mem), lat), device_id_type=MESH)

    def total_of(squares):
        return jnp.sum(squares.reshape(-1, 8, LANES), axis=0)

    zero = jnp.zeros(halo.shape[2:], jnp.float32)

    def start_body(c, carry):
        halo[1, c] = control[c]
        w[c] = control[c]
        send_both(g_copy, c)
        return carry

    lax.fori_loop(0, chunks, start_body, 0)

    @pl.when(jnp.logical_not(has_up))
    def _():
        for c in range(chunks):
            halo[0, c] = zero
            part_recv[1, c] = zero

    @pl.when(jnp.logical_not(has_down))
    def _():
        for c in range(chunks):
            halo[2, c] = zero
            part_recv[0, c] = zero

    for t in range(tiles):
        for v in range(n_vars):
            obs[pl.ds(t * tile_rows + v * fine, fine), :] = innov[v, :, t * LANES:(t + 1) * LANES]

    for c in range(chunks):
        pert_copy(c).wait()
    forward_all()
    reduce_scatter()
    gather_start()
    gather_wait()
    inc[...] = gather[: tiles * tile_rows, :]

    def step(it, carry):
        for t in range(tiles):
            for v in range(n_vars):
                rows = pl.ds(t * tile_rows + v * fine, fine)
                misfit[rows, :] = jnp.clip(inc[rows, :] - obs[rows, :], -thr[v], thr[v])

        def adjoint_body(c, carry):
            adjoint_chunk(c)
            send_both(c_copy, c)
            return carry

        lax.fori_loop(0, chunks, adjoint_body, 0)

        def gradient_body(c, squares):
            recv_both(c_copy, c)
            grad = w[c] + own[c] + part_recv[0, c] + part_recv[1, c]
            halo[1, c] = grad
            send_both(g_copy, c)
            sent_both(c_copy, c)
            return squares + total_of(grad * grad)

        grad_sq = lax.fori_loop(0, chunks, gradient_body, jnp.zeros((8, LANES), jnp.float32))
        forward_all()
        piece = reduce_scatter()
        gather_start()
        image_sq = total_of(piece * piece)
        row = lax.broadcasted_iota(jnp.int32, (8, LANES), 0)
        sums = jnp.where(
            row == 0, jnp.sum(grad_sq, axis=0, keepdims=True),
            jnp.where(row == 1, jnp.sum(image_sq, axis=0, keepdims=True), 0.0))
        sc_lat_send[...] = sums
        for k in range(1, n_lat):
            sl_copy(it, k).start()
        for k in range(1, n_lat):
            sl_copy(it, k).wait_recv()
        for k in range(1, n_lat):
            sums = sums + sc_lat[it, k - 1]
        sc_mem_send[...] = sums
        for k in range(1, n_mem):
            sm_copy(it, k).start()
        for k in range(1, n_mem):
            sm_copy(it, k).wait_recv()
        for k in range(1, n_mem):
            sums = sums + sc_mem[it, k - 1]
        g2 = jnp.sum(sums[0:1, :], axis=1, keepdims=True)
        h2 = jnp.sum(sums[1:2, :], axis=1, keepdims=True)
        step_len = g2 / (g2 + h2)
        for c in range(chunks):
            w[c] = w[c] - step_len * halo[1, c]
        gather_wait()
        inc[...] = inc[...] - step_len * gather[: tiles * tile_rows, :]
        for k in range(1, n_lat):
            sl_copy(it, k).wait_send()
        for k in range(1, n_mem):
            sm_copy(it, k).wait_send()
        return carry

    lax.fori_loop(0, STEPS, step, 0)
    weights_out[...] = w[...]
    inc_out[...] = inc[...]


def per_device(n_mem, n_lat, perturbations, control, innovations, thresholds):
    members, coarse_rows, coarse_cols = control.shape
    n_vars, fine_rows, fine_cols = innovations.shape
    chunks = members // GROUP
    seg = GROUP * coarse_rows
    packed = seg * coarse_cols // LANES
    half = seg // 2
    tail = coarse_cols - 2 * LANES
    flat = n_vars * fine_rows * fine_cols // LANES
    part = -(-flat // n_mem // 8) * 8
    ordered = control.reshape(chunks, GROUP, coarse_rows, coarse_cols).transpose(0, 2, 1, 3).reshape(chunks, seg, coarse_cols)
    ends = ordered[:, :, 2 * LANES:]
    ordered = jnp.concatenate(
        [ordered[:, :, :LANES], ordered[:, :, LANES:2 * LANES], jnp.concatenate([ends[:, :half], ends[:, half:]], axis=2)], axis=1)
    vmem = pl.BlockSpec(memory_space=pltpu.VMEM)
    f32 = jnp.float32
    dma = pltpu.SemaphoreType.DMA
    weights, increment = pl.pallas_call(
        functools.partial(kernel, n_mem, n_lat, seg),
        out_shape=(jax.ShapeDtypeStruct((chunks, packed, LANES), f32), jax.ShapeDtypeStruct((flat, LANES), f32)),
        in_specs=[pl.BlockSpec(memory_space=pl.ANY), vmem, vmem, pl.BlockSpec(memory_space=pltpu.SMEM)] + [vmem] * 6,
        out_specs=(vmem, vmem),
        scratch_shapes=[
            pltpu.VMEM(perturbations.shape, jnp.bfloat16),
            pltpu.VMEM((3, chunks, packed, LANES), f32),
            pltpu.VMEM((2, chunks, packed, LANES), f32),
            pltpu.VMEM((2, chunks, packed, LANES), f32),
            pltpu.VMEM((chunks, packed, LANES), f32),
            pltpu.VMEM((chunks, packed, LANES), f32),
            pltpu.VMEM((n_mem * part, LANES), f32),
            pltpu.VMEM((n_mem * part, LANES), f32),
            pltpu.VMEM((flat, LANES), f32),
            pltpu.VMEM((flat, LANES), f32),
            pltpu.VMEM((flat, LANES), f32),
            pltpu.VMEM((n_mem - 1, part, LANES), f32),
            pltpu.VMEM((8, LANES), f32),
            pltpu.VMEM((STEPS, n_lat - 1, 8, LANES), f32),
            pltpu.VMEM((8, LANES), f32),
            pltpu.VMEM((STEPS, n_mem - 1, 8, LANES), f32),
            dma((chunks,)),
            dma((2, chunks)), dma((2, chunks)), dma((2, chunks)), dma((2, chunks)),
            dma((n_mem - 1,)), dma((n_mem - 1,)), dma((n_mem - 1,)), dma((n_mem - 1,)),
            dma((STEPS, n_lat - 1)), dma((STEPS, n_lat - 1)), dma((STEPS, n_mem - 1)), dma((STEPS, n_mem - 1)),
        ],
        compiler_params=pltpu.CompilerParams(collective_id=0, has_side_effects=True),
    )(perturbations, ordered, innovations, thresholds, *tables(coarse_rows))
    ends = weights[:, 2 * seg:]
    ends = jnp.concatenate([ends[:, :, :tail], ends[:, :, tail:]], axis=1)
    weights = jnp.concatenate([weights[:, :seg], weights[:, seg:2 * seg], ends], axis=2)
    weights = weights.reshape(chunks, coarse_rows, GROUP, coarse_cols).transpose(0, 2, 1, 3).reshape(members, coarse_rows, coarse_cols)
    increment = increment.reshape(fine_cols // LANES, n_vars, fine_rows, LANES).transpose(1, 2, 0, 3).reshape(n_vars, fine_rows, fine_cols)
    share = fine_cols // n_mem
    increment = lax.dynamic_slice_in_dim(increment, lax.axis_index("mem") * share, share, 2)
    return weights, increment


def solution(mesh):
    return jax.shard_map(
        functools.partial(per_device, mesh.shape["mem"], mesh.shape["lat"]),
        mesh=mesh,
        in_specs=(P("mem", None, "lat", None), P("mem", "lat", None), P(None, "lat", None), P()),
        out_specs=(P("mem", "lat", None), P(None, "lat", "mem")),
        check_vma=False,
    )
```

```python
import functools

import jax
import jax.numpy as jnp
import numpy as np
from jax import lax
from jax.experimental import pallas as pl
from jax.experimental.pallas import tpu as pltpu
from jax.sharding import PartitionSpec as P

RATIO = 4
HALF = 5
STEPS = 2
GROUP = 8
PAIR = 2
LANES = 128
MESH = pl.DeviceIdType.MESH
SCALE = 96.0


def tent(distance):
    return np.maximum(0.0, 1.0 - np.abs(distance) / RATIO)


def row_operator(coarse_rows, first, last):
    fine = np.arange(RATIO * coarse_rows)[:, None]
    inner = np.arange(-1, coarse_rows + 1)
    up = tent(fine + 0.5 - RATIO * inner[None, :] - RATIO / 2)
    if first:
        up[:, 0] = 0.0
    if last:
        up[:, -1] = 0.0
    outer = np.arange(-coarse_rows, 2 * coarse_rows)
    gap = np.abs(inner[:, None] - outer[None, :])
    smooth = np.where(gap <= HALF, (1.0 - gap / (HALF + 1)) / 2, 0.0)
    return np.rint(SCALE * up @ smooth)


def block_rows(operator):
    fine, wide = operator.shape
    out = np.zeros((GROUP, fine, wide, GROUP))
    for member in range(GROUP):
        out[member, :, :, member] = operator
    return out.reshape(GROUP * fine, wide * GROUP)


def tables(coarse_rows):
    ops = [block_rows(row_operator(coarse_rows, *ends)) for ends in ((True, False), (False, False), (False, True))]
    rows_up = np.stack(ops)
    rows_down = np.stack([op.T for op in ops])
    fine = np.arange(2 * LANES)[None, :]
    narrow = tent(LANES + fine + 0.5 - RATIO * np.arange(LANES)[:, None] - RATIO / 2)
    wide = tent(3 * LANES + fine + 0.5 - RATIO * np.arange(2 * LANES)[:, None] - RATIO / 2)
    narrow_up = np.concatenate([narrow, narrow], 0)
    wide_up = np.concatenate([wide[:LANES], wide[:LANES], wide[LANES:], wide[LANES:]], 0)
    narrow_down = np.concatenate([narrow.T, narrow.T], 0)
    wide_down = np.concatenate([wide.T, wide.T], 0)
    return [jnp.asarray(t, jnp.bfloat16) for t in (rows_up, rows_down, narrow_up, wide_up, narrow_down, wide_down)]


def split(x):
    high = x.astype(jnp.bfloat16)
    return high, (x - high.astype(jnp.float32)).astype(jnp.bfloat16)


def dot(a, b):
    return jnp.dot(a, b, preferred_element_type=jnp.float32)


def kernel(
    n_mem, n_lat, seg, layout,
    pert_hbm, control_hbm, innov_hbm, thr, rows_up_hbm, rows_down_hbm, narrow_up_hbm, wide_up_hbm, narrow_down_hbm, wide_down_hbm,
    weights_out, inc_out,
    pert_raw, pert, control, innov, rows_up, rows_down, narrow_up, wide_up, narrow_down, wide_down,
    halo, part_send, part_recv, own, w, spare, lifted, acc, pair_recv, half_sum, z_recv, image, inc, misfit, obs,
    lat_send, lat_recv, mem_send, mem_recv,
    pert_sem, load_sem, g_send, g_recv, c_send, c_recv, p_ss, p_rs, z_ss, z_rs, ag_ss, ag_rs, im_ss, im_rs, sl_ss, sl_rs, sm_ss, sm_rs,
):
    mem = lax.axis_index("mem")
    lat = lax.axis_index("lat")
    core = lax.rem(mem, 2)
    n_z = n_mem // 2
    z = mem // 2
    blocks = pert.shape[0] // GROUP
    chunks = blocks // PAIR
    n_vars = pert.shape[1]
    fine = pert.shape[2]
    tiles = pert.shape[3] // LANES
    pairs = tiles // 2
    tile_rows = n_vars * fine
    half = seg // 2
    n_rows = seg // GROUP
    case = jnp.where(lat == 0, 0, jnp.where(lat == n_lat - 1, 2, 1))
    up_id = (mem, jnp.maximum(lat - 1, 0))
    down_id = (mem, jnp.minimum(lat + 1, n_lat - 1))
    has_up = lat > 0
    has_down = lat < n_lat - 1
    partner = (2 * z + 1 - core, lat)
    z_peers = [(2 * lax.rem(z + k, n_z) + core, lat) for k in range(1, n_z)]
    mem_peers = [(lax.rem(mem + k, n_mem), lat) for k in range(1, n_mem)]
    lat_peers = [(mem, lax.rem(lat + k, n_lat)) for k in range(1, n_lat)]
    groups = ((0, seg), (seg, seg + half))
    tail_rows = pl.ds(2 * seg, half)
    bases, parts, starts = layout
    z_bases = [sum(parts[:i]) for i in range(3)]

    loads = [
        (control_hbm, control), (rows_up_hbm.at[case], rows_up), (narrow_up_hbm, narrow_up), (wide_up_hbm, wide_up),
        (innov_hbm, innov), (rows_down_hbm.at[case], rows_down), (narrow_down_hbm, narrow_down), (wide_down_hbm, wide_down),
    ]
    loads = [pltpu.make_async_copy(src, dst, load_sem.at[i]) for i, (src, dst) in enumerate(loads)]

    loads[0].start()
    barrier = pltpu.get_barrier_semaphore()
    for peer in lat_peers + mem_peers:
        pl.semaphore_signal(barrier, inc=1, device_id=peer, device_id_type=MESH)

    def pert_copy(c):
        rows = pl.ds(c * GROUP, GROUP)
        return pltpu.make_async_copy(pert_hbm.at[rows], pert_raw.at[rows], pert_sem.at[c])

    for load in loads[1:4]:
        load.start()
    for c in range(blocks):
        pert_copy(c).start()
    for load in loads[4:]:
        load.start()

    lane = lax.broadcasted_iota(jnp.int32, (half, LANES), 1)
    left = lane < LANES // 2

    def swap(x):
        return pltpu.roll(x, LANES // 2, 1)

    def g_copy(q, b, up):
        rows = pl.ds(*groups[q])
        i = 0 if up else 1
        return pltpu.make_async_remote_copy(
            src_ref=halo.at[1, b, rows], dst_ref=halo.at[2 if up else 0, b, rows],
            send_sem=g_send.at[i, q, b], recv_sem=g_recv.at[i, q, b],
            device_id=up_id if up else down_id, device_id_type=MESH)

    def c_copy(q, b, up):
        rows = pl.ds(*groups[q])
        i = 0 if up else 1
        return pltpu.make_async_remote_copy(
            src_ref=part_send.at[i, b, rows], dst_ref=part_recv.at[i, b, rows],
            send_sem=c_send.at[i, q, b], recv_sem=c_recv.at[i, q, b],
            device_id=up_id if up else down_id, device_id_type=MESH)

    def send_both(copy, q, bs):
        @pl.when(has_up)
        def _():
            for b in bs:
                copy(q, b, True).start()

        @pl.when(has_down)
        def _():
            for b in bs:
                copy(q, b, False).start()

    def recv_both(copy, q, bs):
        @pl.when(has_down)
        def _():
            for b in bs:
                copy(q, b, True).wait_recv()

        @pl.when(has_up)
        def _():
            for b in bs:
                copy(q, b, False).wait_recv()

    def sent_all(copy):
        def body(b, carry):
            for q in range(2):
                @pl.when(has_up)
                def _():
                    copy(q, b, True).wait_send()

                @pl.when(has_down)
                def _():
                    copy(q, b, False).wait_send()
            return carry

        lax.fori_loop(0, blocks, body, 0)

    def over_chunks(f):
        def body(c, carry):
            f([c * PAIR + i for i in range(PAIR)])
            return carry

        lax.fori_loop(0, chunks, body, 0)

    def lane_pair(j):
        return 2 * j + 1, (2 * j + 2) % tiles

    def flat_rows(j, v):
        return pl.ds(starts[j] + v * fine, fine)

    def both_pieces(x):
        high, low = split(x)
        return jnp.concatenate([high, low], axis=1)

    def lift(g, b):
        pieces = []
        for i in range(3):
            if g < 2:
                pieces.append(halo[i, b, pl.ds(g * seg, seg), :])
            else:
                first = halo[i, b, pl.ds(0, seg), :]
                tail = halo[i, b, tail_rows, :]
                pieces.append(jnp.where(left, tail, swap(first[:half])))
                pieces.append(jnp.where(left, swap(tail), swap(first[half:])))
        wide = dot(rows_up[...], both_pieces(jnp.concatenate(pieces, axis=0)))
        return both_pieces(wide[:, :LANES] + wide[:, LANES:])

    def accumulate(j, bs, fields):
        for h, t in enumerate(lane_pair(j)):
            for v in range(n_vars):
                total = acc[h, flat_rows(j, v), :]
                for b, field in zip(bs, fields):
                    f = field[:, h * LANES:(h + 1) * LANES].reshape(GROUP, fine, LANES)
                    p = pert[pl.ds(b * GROUP, GROUP), v, :, t * LANES:(t + 1) * LANES]
                    total = total + jnp.sum(p * f, axis=0)
                acc[h, flat_rows(j, v), :] = total

    def forward_first(bs):
        recv_both(g_copy, 0, bs)
        new = [lift(0, b) for b in bs]
        for b, value in zip(bs, new):
            lifted[b] = value
        accumulate(0, bs, [dot(value, narrow_up[...]) for value in new])

    def odd_tile(a, b):
        return dot(a, wide_up[:2 * LANES, :]) + dot(b, wide_up[2 * LANES:, :])

    def forward_second(b, split_at=None):
        recv_both(g_copy, 1, [b])
        one, two = lift(1, b), lift(2, b)
        accumulate(1, [b], [odd_tile(lifted[b], one)])
        accumulate(2, [b], [dot(one, narrow_up[...])])
        if split_at is not None:
            split_at()
        accumulate(3, [b], [odd_tile(one, two)])
        accumulate(4, [b], [dot(two, narrow_up[...])])

    def weighted(j, b):
        pieces = []
        for h, t in enumerate(lane_pair(j)):
            total = None
            for v in range(n_vars):
                p = pert[pl.ds(b * GROUP, GROUP), v, :, t * LANES:(t + 1) * LANES]
                term = p * misfit[h, flat_rows(j, v), :][None]
                total = term if total is None else total + term
            pieces.append(split(total.reshape(GROUP * fine, LANES)))
        lhs = jnp.concatenate([pieces[0][0], pieces[1][0], pieces[0][1], pieces[1][1]], axis=1)
        return dot(lhs, narrow_down[...] if j % 2 == 0 else wide_down[...])

    def lower(x):
        wide = dot(rows_down[...], both_pieces(x))
        return (wide[:, :LANES] + wide[:, LANES:]) * (1.0 / SCALE)

    def keep(b, rows, coarse):
        part_send[0, b, rows, :] = coarse[0]
        own[b, rows, :] = coarse[1]
        part_send[1, b, rows, :] = coarse[2]

    def three(x):
        return x[:seg], x[seg:2 * seg], x[2 * seg:]

    def adjoint_first(bs):
        for b in bs:
            last = weighted(4, b)
            wide = weighted(1, b)
            wrapped = jnp.where(lax.broadcasted_iota(jnp.int32, last.shape, 1) < LANES // 2, swap(last), 0.0)
            first = weighted(0, b) + wide[:, :LANES] + wrapped
            spare[b, 0] = wide[:, LANES:]
            spare[b, 1] = last
            keep(b, pl.ds(0, seg), three(lower(first)))
        send_both(c_copy, 0, bs)

    def adjoint_second(bs):
        for b in bs:
            wide = weighted(3, b)
            keep(b, pl.ds(seg, seg), three(lower(spare[b, 0] + weighted(2, b) + wide[:, :LANES])))
            ends = three(lower(spare[b, 1] + wide[:, LANES:]))
            keep(b, tail_rows, [jnp.where(left, e[:half], swap(e[half:])) for e in ends])
        send_both(c_copy, 1, bs)

    def region(s):
        return pl.ds(bases[s], n_z * parts[s])

    def part_rows(s, at):
        return pl.ds(pl.multiple_of(bases[s] + at * parts[s], 8), parts[s])

    def pair_copy(s):
        return pltpu.make_async_remote_copy(
            src_ref=acc.at[1 - core, region(s)], dst_ref=pair_recv.at[region(s)],
            send_sem=p_ss.at[s], recv_sem=p_rs.at[s], device_id=partner, device_id_type=MESH)

    def z_copy(s, k):
        return pltpu.make_async_remote_copy(
            src_ref=half_sum.at[part_rows(s, lax.rem(z + k + 1, n_z))], dst_ref=z_recv.at[k, pl.ds(z_bases[s], parts[s])],
            send_sem=z_ss.at[s, k], recv_sem=z_rs.at[s, k], device_id=z_peers[k], device_id_type=MESH)

    def ag_copy(s, k, source):
        return pltpu.make_async_remote_copy(
            src_ref=image.at[core, part_rows(s, source)], dst_ref=image.at[core, part_rows(s, source)],
            send_sem=ag_ss.at[s, k], recv_sem=ag_rs.at[s, k], device_id=z_peers[k], device_id_type=MESH)

    def image_copy(index):
        return pltpu.make_async_remote_copy(
            src_ref=image.at[index], dst_ref=image.at[index],
            send_sem=im_ss.at[0], recv_sem=im_rs.at[0], device_id=partner, device_id_type=MESH)

    def pair_finish(s):
        pair_copy(s).wait_recv()
        half_sum[region(s), :] = acc[core, region(s), :] + pair_recv[region(s), :]
        for k in range(n_z - 1):
            z_copy(s, k).start()

    def z_finish(s):
        for k in range(n_z - 1):
            z_copy(s, k).wait_recv()
        total = half_sum[part_rows(s, z), :]
        for k in range(n_z - 1):
            total = total + z_recv[k, pl.ds(z_bases[s], parts[s]), :]
        total = total * (1.0 / SCALE)
        image[core, part_rows(s, z), :] = total
        if s < 2:
            gather_start(s)
        return total_of(total * total)

    def gather_start(s):
        for k in range(n_z - 1):
            ag_copy(s, k, z).start()

    def gather_pass():
        for s in range(3):
            for k in range(n_z - 1):
                ag_copy(s, k, lax.rem(z + n_z - 1 - k, n_z)).wait_recv()
        image_copy(core).start()

    def gather_finish():
        image_copy(1 - core).wait_recv()
        image_copy(core).wait_send()
        for s in range(3):
            pair_copy(s).wait_send()
            for k in range(n_z - 1):
                z_copy(s, k).wait_send()
                ag_copy(s, k, z).wait_send()

    def total_of(squares):
        return jnp.sum(squares.reshape(-1, 8, LANES), axis=0)

    def forward_all():
        acc[...] = jnp.zeros_like(acc)
        over_chunks(forward_first)
        pair_copy(0).start()

        def body(b, carry):
            forward_second(b)
            return carry

        forward_second(0)
        pair_finish(0)
        lax.fori_loop(1, blocks - 1, body, 0)
        forward_second(blocks - 1, lambda: pair_copy(1).start())
        pair_copy(2).start()
        pair_finish(1)
        pair_finish(2)
        squares = z_finish(0)
        squares = squares + z_finish(1)
        squares = squares + z_finish(2)
        return squares

    def sl_copy(it, k):
        return pltpu.make_async_remote_copy(
            src_ref=lat_send, dst_ref=lat_recv.at[it, k],
            send_sem=sl_ss.at[it, k], recv_sem=sl_rs.at[it, k], device_id=lat_peers[k], device_id_type=MESH)

    def sm_copy(it, k):
        return pltpu.make_async_remote_copy(
            src_ref=mem_send, dst_ref=mem_recv.at[it, k],
            send_sem=sm_ss.at[it, k], recv_sem=sm_rs.at[it, k], device_id=mem_peers[k], device_id_type=MESH)

    loads[0].wait()
    for b in range(blocks):
        block = control[:, pl.ds(b * GROUP, GROUP), :].reshape(seg, control.shape[2])
        ends = block[:, 2 * LANES:]
        tail = jnp.concatenate([ends[:half], ends[half:]], axis=1)
        for rows, value in ((pl.ds(0, seg), block[:, :LANES]), (pl.ds(seg, seg), block[:, LANES:2 * LANES]), (pl.ds(2 * seg, half), tail)):
            halo[1, b, rows, :] = value
            w[b, rows, :] = value

    pl.semaphore_wait(barrier, len(lat_peers) + len(mem_peers))
    over_chunks(functools.partial(send_both, g_copy, 0))
    over_chunks(functools.partial(send_both, g_copy, 1))

    zero = jnp.zeros(halo.shape[2:], jnp.float32)

    @pl.when(jnp.logical_not(has_up))
    def _():
        for b in range(blocks):
            halo[0, b] = zero
            part_recv[1, b] = zero

    @pl.when(jnp.logical_not(has_down))
    def _():
        for b in range(blocks):
            halo[2, b] = zero
            part_recv[0, b] = zero

    for load in loads[1:]:
        load.wait()
    for j in range(pairs):
        for h, t in enumerate(lane_pair(j)):
            for v in range(n_vars):
                obs[h, flat_rows(j, v), :] = innov[v, :, t * LANES:(t + 1) * LANES]
    for c in range(blocks):
        pert_copy(c).wait()

    def widen(m, carry):
        pert[m] = pert_raw[m].astype(jnp.float32)
        return carry

    lax.fori_loop(0, pert.shape[0], widen, 0)
    forward_all()
    gather_start(2)
    sent_all(g_copy)
    gather_pass()
    gather_finish()
    inc[...] = image[...]

    def step(it, carry):
        for h in range(2):
            for j in range(pairs):
                for v in range(n_vars):
                    rows = flat_rows(j, v)
                    misfit[h, rows, :] = jnp.clip(inc[h, rows, :] - obs[h, rows, :], -thr[v], thr[v])
        over_chunks(adjoint_first)
        over_chunks(adjoint_second)

        def gradient(q):
            def body(b, squares):
                recv_both(c_copy, q, [b])
                rows = pl.ds(*groups[q])
                grad = w[b, rows, :] + own[b, rows, :] + part_recv[0, b, rows, :] + part_recv[1, b, rows, :]
                halo[1, b, rows, :] = grad
                send_both(g_copy, q, [b])
                return squares + total_of(grad * grad)

            return lax.fori_loop(0, blocks, body, jnp.zeros((8, LANES), jnp.float32))

        grad_sq = gradient(0)
        grad_sq = grad_sq + gradient(1)
        image_sq = forward_all()
        sums = jnp.concatenate([jnp.sum(grad_sq, axis=0, keepdims=True), jnp.sum(image_sq, axis=0, keepdims=True)], axis=0)
        lat_send[...] = sums
        for k in range(n_lat - 1):
            sl_copy(it, k).start()
        gather_start(2)
        sent_all(c_copy)
        sent_all(g_copy)
        gather_pass()
        for k in range(n_lat - 1):
            sl_copy(it, k).wait_recv()
        sums = sums + jnp.sum(lat_recv[it], axis=0)
        mem_send[...] = sums
        for k in range(n_mem - 1):
            sm_copy(it, k).start()
        for k in range(n_lat - 1):
            sl_copy(it, k).wait_send()
        gather_finish()
        for k in range(n_mem - 1):
            sm_copy(it, k).wait_recv()
        sums = sums + jnp.sum(mem_recv[it], axis=0)
        g2 = jnp.sum(sums[0:1, :], axis=1, keepdims=True)
        h2 = jnp.sum(sums[1:2, :], axis=1, keepdims=True)
        step_len = g2 / (g2 + h2)
        inc[...] = inc[...] - step_len[None] * image[...]
        for b in range(blocks):
            w[b] = w[b] - step_len * halo[1, b]
        for k in range(n_mem - 1):
            sm_copy(it, k).wait_send()
        return carry

    lax.fori_loop(0, STEPS, step, 0)

    for b in range(blocks):
        members = pl.ds(b * GROUP, GROUP)
        tail = w[b, pl.ds(2 * seg, half), :]
        weights_out[:, members, :LANES] = w[b, pl.ds(0, seg), :].reshape(n_rows, GROUP, LANES)
        weights_out[:, members, LANES:2 * LANES] = w[b, pl.ds(seg, seg), :].reshape(n_rows, GROUP, LANES)
        weights_out[:n_rows // 2, members, 2 * LANES:] = tail[:, :LANES // 2].reshape(n_rows // 2, GROUP, LANES // 2)
        weights_out[n_rows // 2:, members, 2 * LANES:] = tail[:, LANES // 2:].reshape(n_rows // 2, GROUP, LANES // 2)

    share = inc_out.shape[2]
    first = mem * share // LANES
    shift = mem * share - first * LANES

    def lane_tile(t, v):
        j = jnp.where(t % 2 == 1, (t - 1) // 2, (t // 2 + pairs - 1) % pairs)
        row = jnp.int32(0)
        for i in range(pairs):
            row = jnp.where(j == i, starts[i] + v * fine, row)
        return inc[1 - t % 2, pl.ds(pl.multiple_of(row, 8), fine), :]

    fine_lane = lax.broadcasted_iota(jnp.int32, (fine, LANES), 1)
    for v in range(n_vars):
        a = pltpu.roll(lane_tile(first, v), (LANES - shift) % LANES, 1)
        b = pltpu.roll(lane_tile(first + 1, v), (LANES - shift) % LANES, 1)
        inc_out[v, :, :LANES] = jnp.where(fine_lane < LANES - shift, a, b)
        inc_out[v, :, LANES:] = b[:, :share - LANES]


def per_device(n_mem, n_lat, perturbations, control, innovations, thresholds):
    members, coarse_rows, coarse_cols = control.shape
    n_vars, fine_rows, fine_cols = innovations.shape
    blocks = members // GROUP
    seg = GROUP * coarse_rows
    packed = seg * coarse_cols // LANES
    n_z = n_mem // 2
    tile_rows = n_vars * fine_rows
    pairs = fine_cols // (2 * LANES)
    parts, bases, starts, flat = [], [], [], 0
    for count in (1, 2, pairs - 3):
        parts.append(-(-count * tile_rows // n_z // 8) * 8)
        bases.append(flat)
        starts += [flat + i * tile_rows for i in range(count)]
        flat += n_z * parts[-1]
    vmem = pl.BlockSpec(memory_space=pltpu.VMEM)
    whole = pl.BlockSpec(memory_space=pl.ANY)
    f32 = jnp.float32
    bf16 = jnp.bfloat16
    dma = pltpu.SemaphoreType.DMA
    constants = tables(coarse_rows)
    ordered = control.transpose(1, 0, 2)
    shapes = (
        jax.ShapeDtypeStruct(ordered.shape, f32),
        jax.ShapeDtypeStruct((n_vars, fine_rows, fine_cols // n_mem), f32))
    weights, increment = pl.pallas_call(
        functools.partial(kernel, n_mem, n_lat, seg, (bases, parts, starts)),
        out_shape=tuple(pltpu.VMEM(x.shape, f32) for x in shapes),
        in_specs=[whole, whole, whole, pl.BlockSpec(memory_space=pltpu.SMEM)] + [whole] * 6,
        out_specs=(vmem, vmem),
        scratch_shapes=[
            pltpu.VMEM(perturbations.shape, bf16),
            pltpu.VMEM(perturbations.shape, f32),
            pltpu.VMEM(ordered.shape, f32),
            pltpu.VMEM(innovations.shape, f32),
            pltpu.VMEM(constants[0].shape[1:], bf16),
            pltpu.VMEM(constants[1].shape[1:], bf16),
            pltpu.VMEM(constants[2].shape, bf16),
            pltpu.VMEM(constants[3].shape, bf16),
            pltpu.VMEM(constants[4].shape, bf16),
            pltpu.VMEM(constants[5].shape, bf16),
            pltpu.VMEM((3, blocks, packed, LANES), f32),
            pltpu.VMEM((2, blocks, packed, LANES), f32),
            pltpu.VMEM((2, blocks, packed, LANES), f32),
            pltpu.VMEM((blocks, packed, LANES), f32),
            pltpu.VMEM((blocks, packed, LANES), f32),
            pltpu.VMEM((blocks, 2, GROUP * fine_rows, LANES), f32),
            pltpu.VMEM((blocks, GROUP * fine_rows, 2 * LANES), bf16),
            pltpu.VMEM((2, flat, LANES), f32),
            pltpu.VMEM((flat, LANES), f32),
            pltpu.VMEM((flat, LANES), f32),
            pltpu.VMEM((n_z - 1, sum(parts), LANES), f32),
            pltpu.VMEM((2, flat, LANES), f32),
            pltpu.VMEM((2, flat, LANES), f32),
            pltpu.VMEM((2, flat, LANES), f32),
            pltpu.VMEM((2, flat, LANES), f32),
            pltpu.VMEM((2, LANES), f32),
            pltpu.VMEM((STEPS, n_lat - 1, 2, LANES), f32),
            pltpu.VMEM((2, LANES), f32),
            pltpu.VMEM((STEPS, n_mem - 1, 2, LANES), f32),
            dma((blocks,)), dma((8,)),
            dma((2, 2, blocks)), dma((2, 2, blocks)), dma((2, 2, blocks)), dma((2, 2, blocks)),
            dma((3,)), dma((3,)), dma((3, n_z - 1)), dma((3, n_z - 1)), dma((3, n_z - 1)), dma((3, n_z - 1)), dma((1,)), dma((1,)),
            dma((STEPS, n_lat - 1)), dma((STEPS, n_lat - 1)), dma((STEPS, n_mem - 1)), dma((STEPS, n_mem - 1)),
        ],
        compiler_params=pltpu.CompilerParams(collective_id=0, has_side_effects=True),
    )(perturbations, ordered, innovations, thresholds, *constants)
    return weights.transpose(1, 0, 2), increment


def solution(mesh):
    return jax.shard_map(
        functools.partial(per_device, mesh.shape["mem"], mesh.shape["lat"]),
        mesh=mesh,
        in_specs=(P("mem", None, "lat", None), P("mem", "lat", None), P(None, "lat", None), P()),
        out_specs=(P("mem", "lat", None), P(None, "lat", "mem")),
        check_vma=False,
    )
```

```python
import functools

import jax
import jax.numpy as jnp
import numpy as np
from jax import lax
from jax.experimental import pallas as pl
from jax.experimental.pallas import tpu as pltpu
from jax.sharding import PartitionSpec as P

RATIO = 4
HALF = 5
STEPS = 2
SIDE = 4
GROUP = 8
PAIR = 2
LANES = 128
MESH = pl.DeviceIdType.MESH
SCALE = 96.0


def tent(distance):
    return np.maximum(0.0, 1.0 - np.abs(distance) / RATIO)


def row_operator(coarse_rows, first, last):
    fine = np.arange(RATIO * coarse_rows)[:, None]
    inner = np.arange(-1, coarse_rows + 1)
    up = tent(fine + 0.5 - RATIO * inner[None, :] - RATIO / 2)
    if first:
        up[:, 0] = 0.0
    if last:
        up[:, -1] = 0.0
    outer = np.arange(-coarse_rows, 2 * coarse_rows)
    gap = np.abs(inner[:, None] - outer[None, :])
    smooth = np.where(gap <= HALF, (1.0 - gap / (HALF + 1)) / 2, 0.0)
    return np.rint(SCALE * up @ smooth)


def block_rows(operator):
    fine, wide = operator.shape
    out = np.zeros((GROUP, fine, wide, GROUP))
    for member in range(GROUP):
        out[member, :, :, member] = operator
    return out.reshape(GROUP * fine, wide * GROUP)


def tables(coarse_rows):
    ops = [block_rows(row_operator(coarse_rows, *ends)) for ends in ((True, False), (False, False), (False, True))]
    rows_up = np.stack(ops)
    rows_down = np.stack([op.T for op in ops])
    fine = np.arange(2 * LANES)[None, :]
    narrow = tent(LANES + fine + 0.5 - RATIO * np.arange(LANES)[:, None] - RATIO / 2)
    wide = tent(3 * LANES + fine + 0.5 - RATIO * np.arange(2 * LANES)[:, None] - RATIO / 2)
    narrow_up = np.concatenate([narrow, narrow], 0)
    wide_up = np.concatenate([wide[:LANES], wide[:LANES], wide[LANES:], wide[LANES:]], 0)
    narrow_down = np.concatenate([narrow.T, narrow.T], 0)
    wide_down = np.concatenate([wide.T, wide.T], 0)
    return [jnp.asarray(t, jnp.bfloat16) for t in (rows_up, rows_down, narrow_up, wide_up, narrow_down, wide_down)]


def split(x):
    high = x.astype(jnp.bfloat16)
    return high, (x - high.astype(jnp.float32)).astype(jnp.bfloat16)


def dot(a, b):
    return jnp.dot(a, b, preferred_element_type=jnp.float32)


def kernel(
    n_mem, n_lat, seg, layout,
    pert_hbm, control_hbm, innov_hbm, thr, rows_up_hbm, rows_down_hbm, narrow_up_hbm, wide_up_hbm, narrow_down_hbm, wide_down_hbm,
    weights_out, inc_out,
    pert_raw, pert, control, innov, rows_up, rows_down, narrow_up, wide_up, narrow_down, wide_down,
    halo, part_send, part_recv, own, w, spare, lifted, acc, pair_recv, half_sum, z_recv, image, inc, misfit, obs,
    lat_send, lat_recv, mem_send, mem_recv,
    pert_sem, load_sem, g_send, g_recv, c_send, c_recv, p_ss, p_rs, z_ss, z_rs, ag_ss, ag_rs, im_ss, im_rs, sl_ss, sl_rs, sm_ss, sm_rs,
):
    mem = lax.axis_index("mem")
    lat = lax.axis_index("lat")
    core = lax.rem(mem, 2)
    n_z = n_mem // 2
    z = mem // 2
    blocks = pert.shape[0] // GROUP
    chunks = blocks // PAIR
    n_vars = pert.shape[1]
    fine = pert.shape[2]
    tiles = pert.shape[3] // LANES
    pairs = tiles // 2
    tile_rows = n_vars * fine
    half = seg // 2
    n_rows = seg // GROUP
    case = jnp.where(lat == 0, 0, jnp.where(lat == n_lat - 1, 2, 1))
    up_id = (mem, jnp.maximum(lat - 1, 0))
    down_id = (mem, jnp.minimum(lat + 1, n_lat - 1))
    has_up = lat > 0
    has_down = lat < n_lat - 1
    partner = (2 * z + 1 - core, lat)
    z_peers = [(2 * lax.rem(z + k, n_z) + core, lat) for k in range(1, n_z)]
    mem_peers = [(2 * lax.rem(z + k, n_z) + c, lat) for k in (2, 1, 3) for c in (core, 1 - core)] + [partner]
    far = sorted(((i, k) for i in range(SIDE) for k in range(SIDE) if i or k), key=lambda at: -sum(min(d, SIDE - d) for d in at))
    lat_peers = [(mem, lax.rem(lat // SIDE + i, SIDE) * SIDE + lax.rem(lat + k, SIDE)) for i, k in far]
    groups = ((0, seg + half), (seg + half, seg))
    first_rows, tail_rows, second_rows = pl.ds(0, seg), pl.ds(seg, half), pl.ds(seg + half, seg)
    bases, parts, starts = layout
    z_bases = [sum(parts[:i]) for i in range(3)]

    loads = [
        (control_hbm, control), (rows_up_hbm.at[case], rows_up), (narrow_up_hbm, narrow_up), (wide_up_hbm, wide_up),
        (innov_hbm, innov), (rows_down_hbm.at[case], rows_down), (narrow_down_hbm, narrow_down), (wide_down_hbm, wide_down),
    ]
    loads = [pltpu.make_async_copy(src, dst, load_sem.at[i]) for i, (src, dst) in enumerate(loads)]

    loads[0].start()
    barrier = pltpu.get_barrier_semaphore()
    for peer in lat_peers + mem_peers:
        pl.semaphore_signal(barrier, inc=1, device_id=peer, device_id_type=MESH)

    def pert_copy(c):
        rows = pl.ds(c * GROUP, GROUP)
        return pltpu.make_async_copy(pert_hbm.at[rows], pert_raw.at[rows], pert_sem.at[c])

    for load in loads[1:4]:
        load.start()
    for c in range(blocks):
        pert_copy(c).start()
    for load in loads[4:]:
        load.start()

    lane = lax.broadcasted_iota(jnp.int32, (half, LANES), 1)
    left = lane < LANES // 2

    def swap(x):
        return pltpu.roll(x, LANES // 2, 1)

    def g_copy(q, b, up):
        rows = pl.ds(*groups[q])
        i = 0 if up else 1
        return pltpu.make_async_remote_copy(
            src_ref=halo.at[1, b, rows], dst_ref=halo.at[2 if up else 0, b, rows],
            send_sem=g_send.at[i, q, b], recv_sem=g_recv.at[i, q, b],
            device_id=up_id if up else down_id, device_id_type=MESH)

    def c_copy(q, b, up):
        rows = pl.ds(*groups[q])
        i = 0 if up else 1
        return pltpu.make_async_remote_copy(
            src_ref=part_send.at[i, b, rows], dst_ref=part_recv.at[i, b, rows],
            send_sem=c_send.at[i, q, b], recv_sem=c_recv.at[i, q, b],
            device_id=up_id if up else down_id, device_id_type=MESH)

    def send_both(copy, q, bs):
        @pl.when(has_up)
        def _():
            for b in bs:
                copy(q, b, True).start()

        @pl.when(has_down)
        def _():
            for b in bs:
                copy(q, b, False).start()

    def recv_both(copy, q, bs):
        @pl.when(has_down)
        def _():
            for b in bs:
                copy(q, b, True).wait_recv()

        @pl.when(has_up)
        def _():
            for b in bs:
                copy(q, b, False).wait_recv()

    def sent_all(copy):
        def body(b, carry):
            for q in range(2):
                @pl.when(has_up)
                def _():
                    copy(q, b, True).wait_send()

                @pl.when(has_down)
                def _():
                    copy(q, b, False).wait_send()
            return carry

        lax.fori_loop(0, blocks, body, 0)

    def over_chunks(f):
        def body(c, carry):
            f([c * PAIR + i for i in range(PAIR)])
            return carry

        lax.fori_loop(0, chunks, body, 0)

    def lane_pair(j):
        return 2 * j + 1, (2 * j + 2) % tiles

    def flat_rows(j, v):
        return pl.ds(starts[j] + v * fine, fine)

    def both_pieces(x):
        high, low = split(x)
        return jnp.concatenate([high, low], axis=1)

    def lift(g, b):
        pieces = []
        for i in range(3):
            if g < 2:
                pieces.append(halo[i, b, second_rows if g else first_rows, :])
            else:
                first = halo[i, b, first_rows, :]
                tail = halo[i, b, tail_rows, :]
                pieces.append(jnp.where(left, tail, swap(first[:half])))
                pieces.append(jnp.where(left, swap(tail), swap(first[half:])))
        wide = dot(rows_up[...], both_pieces(jnp.concatenate(pieces, axis=0)))
        return both_pieces(wide[:, :LANES] + wide[:, LANES:])

    def accumulate(j, bs, fields):
        for h, t in enumerate(lane_pair(j)):
            for v in range(n_vars):
                total = acc[h, flat_rows(j, v), :]
                for b, field in zip(bs, fields):
                    f = field[:, h * LANES:(h + 1) * LANES].reshape(GROUP, fine, LANES)
                    p = pert[pl.ds(b * GROUP, GROUP), v, :, t * LANES:(t + 1) * LANES]
                    total = total + jnp.sum(p * f, axis=0)
                acc[h, flat_rows(j, v), :] = total

    def forward_first(bs):
        recv_both(g_copy, 0, bs)
        zero_th = [lift(0, b) for b in bs]
        two = [lift(2, b) for b in bs]
        for b, p, q in zip(bs, zero_th, two):
            lifted[b, 0] = p
            lifted[b, 1] = q
        accumulate(0, bs, [dot(value, narrow_up[...]) for value in zero_th])
        accumulate(4, bs, [dot(value, narrow_up[...]) for value in two])

    def odd_tile(a, b):
        return dot(a, wide_up[:2 * LANES, :]) + dot(b, wide_up[2 * LANES:, :])

    def forward_second(b, split_at=None):
        recv_both(g_copy, 1, [b])
        one = lift(1, b)
        accumulate(1, [b], [odd_tile(lifted[b, 0], one)])
        accumulate(2, [b], [dot(one, narrow_up[...])])
        if split_at is not None:
            split_at()
        accumulate(3, [b], [odd_tile(one, lifted[b, 1])])

    def weighted(j, b):
        pieces = []
        for h, t in enumerate(lane_pair(j)):
            total = None
            for v in range(n_vars):
                p = pert[pl.ds(b * GROUP, GROUP), v, :, t * LANES:(t + 1) * LANES]
                term = p * misfit[h, flat_rows(j, v), :][None]
                total = term if total is None else total + term
            pieces.append(split(total.reshape(GROUP * fine, LANES)))
        lhs = jnp.concatenate([pieces[0][0], pieces[1][0], pieces[0][1], pieces[1][1]], axis=1)
        return dot(lhs, narrow_down[...] if j % 2 == 0 else wide_down[...])

    def lower(x):
        wide = dot(rows_down[...], both_pieces(x))
        return (wide[:, :LANES] + wide[:, LANES:]) * (1.0 / SCALE)

    def keep(b, rows, coarse):
        part_send[0, b, rows, :] = coarse[0]
        own[b, rows, :] = coarse[1]
        part_send[1, b, rows, :] = coarse[2]

    def three(x):
        return x[:seg], x[seg:2 * seg], x[2 * seg:]

    def adjoint_first(bs):
        for b in bs:
            last = weighted(4, b)
            wide = weighted(1, b)
            high = weighted(3, b)
            wrapped = jnp.where(lax.broadcasted_iota(jnp.int32, last.shape, 1) < LANES // 2, swap(last), 0.0)
            first = weighted(0, b) + wide[:, :LANES] + wrapped
            spare[b] = wide[:, LANES:] + high[:, :LANES]
            keep(b, first_rows, three(lower(first)))
            ends = three(lower(last + high[:, LANES:]))
            keep(b, tail_rows, [jnp.where(left, e[:half], swap(e[half:])) for e in ends])
        send_both(c_copy, 0, bs)

    def adjoint_second(bs):
        for b in bs:
            keep(b, second_rows, three(lower(spare[b] + weighted(2, b))))
        send_both(c_copy, 1, bs)

    def region(s):
        return pl.ds(bases[s], n_z * parts[s])

    def part_rows(s, at):
        return pl.ds(pl.multiple_of(bases[s] + at * parts[s], 8), parts[s])

    def pair_copy(s):
        return pltpu.make_async_remote_copy(
            src_ref=acc.at[1 - core, region(s)], dst_ref=pair_recv.at[region(s)],
            send_sem=p_ss.at[s], recv_sem=p_rs.at[s], device_id=partner, device_id_type=MESH)

    def z_copy(s, k):
        return pltpu.make_async_remote_copy(
            src_ref=half_sum.at[part_rows(s, lax.rem(z + k + 1, n_z))], dst_ref=z_recv.at[k, pl.ds(z_bases[s], parts[s])],
            send_sem=z_ss.at[s, k], recv_sem=z_rs.at[s, k], device_id=z_peers[k], device_id_type=MESH)

    def ag_copy(s, k, source):
        return pltpu.make_async_remote_copy(
            src_ref=image.at[core, part_rows(s, source)], dst_ref=image.at[core, part_rows(s, source)],
            send_sem=ag_ss.at[s, k], recv_sem=ag_rs.at[s, k], device_id=z_peers[k], device_id_type=MESH)

    def image_copy(index):
        return pltpu.make_async_remote_copy(
            src_ref=image.at[index], dst_ref=image.at[index],
            send_sem=im_ss.at[0], recv_sem=im_rs.at[0], device_id=partner, device_id_type=MESH)

    def pair_finish(s):
        pair_copy(s).wait_recv()
        half_sum[region(s), :] = acc[core, region(s), :] + pair_recv[region(s), :]
        for k in range(n_z - 1):
            z_copy(s, k).start()

    def z_finish(s):
        for k in range(n_z - 1):
            z_copy(s, k).wait_recv()
        total = half_sum[part_rows(s, z), :]
        for k in range(n_z - 1):
            total = total + z_recv[k, pl.ds(z_bases[s], parts[s]), :]
        total = total * (1.0 / SCALE)
        image[core, part_rows(s, z), :] = total
        if s < 2:
            gather_start(s)
        return total_of(total * total)

    def gather_start(s):
        for k in range(n_z - 1):
            ag_copy(s, k, z).start()

    def gather_pass():
        for s in range(3):
            for k in range(n_z - 1):
                ag_copy(s, k, lax.rem(z + n_z - 1 - k, n_z)).wait_recv()
        image_copy(core).start()

    def gather_finish():
        image_copy(1 - core).wait_recv()
        image_copy(core).wait_send()
        for s in range(3):
            pair_copy(s).wait_send()
            for k in range(n_z - 1):
                z_copy(s, k).wait_send()
                ag_copy(s, k, z).wait_send()

    def total_of(squares):
        return jnp.sum(squares.reshape(-1, 8, LANES), axis=0)

    def forward_all():
        acc[...] = jnp.zeros_like(acc)
        over_chunks(forward_first)
        pair_copy(0).start()

        def body(b, carry):
            forward_second(b)
            return carry

        lax.fori_loop(0, blocks - 1, body, 0)
        pair_finish(0)
        forward_second(blocks - 1, lambda: pair_copy(1).start())
        pair_copy(2).start()
        pair_finish(1)
        pair_finish(2)
        squares = z_finish(0)
        squares = squares + z_finish(1)
        squares = squares + z_finish(2)
        return squares

    def sl_copy(it, k):
        return pltpu.make_async_remote_copy(
            src_ref=lat_send, dst_ref=lat_recv.at[it, k],
            send_sem=sl_ss.at[it, k], recv_sem=sl_rs.at[it, k], device_id=lat_peers[k], device_id_type=MESH)

    def sm_copy(it, k):
        return pltpu.make_async_remote_copy(
            src_ref=mem_send, dst_ref=mem_recv.at[it, k],
            send_sem=sm_ss.at[it, k], recv_sem=sm_rs.at[it, k], device_id=mem_peers[k], device_id_type=MESH)

    loads[0].wait()
    for b in range(blocks):
        block = control[:, pl.ds(b * GROUP, GROUP), :].reshape(seg, control.shape[2])
        ends = block[:, 2 * LANES:]
        tail = jnp.concatenate([ends[:half], ends[half:]], axis=1)
        for rows, value in ((first_rows, block[:, :LANES]), (second_rows, block[:, LANES:2 * LANES]), (tail_rows, tail)):
            halo[1, b, rows, :] = value
            w[b, rows, :] = value

    pl.semaphore_wait(barrier, len(lat_peers) + len(mem_peers))
    over_chunks(functools.partial(send_both, g_copy, 0))
    over_chunks(functools.partial(send_both, g_copy, 1))

    zero = jnp.zeros(halo.shape[2:], jnp.float32)

    @pl.when(jnp.logical_not(has_up))
    def _():
        for b in range(blocks):
            halo[0, b] = zero
            part_recv[1, b] = zero

    @pl.when(jnp.logical_not(has_down))
    def _():
        for b in range(blocks):
            halo[2, b] = zero
            part_recv[0, b] = zero

    for load in loads[1:]:
        load.wait()
    for j in range(pairs):
        for h, t in enumerate(lane_pair(j)):
            for v in range(n_vars):
                obs[h, flat_rows(j, v), :] = innov[v, :, t * LANES:(t + 1) * LANES]
    for c in range(blocks):
        pert_copy(c).wait()

    def widen(m, carry):
        pert[m] = pert_raw[m].astype(jnp.float32)
        return carry

    lax.fori_loop(0, pert.shape[0], widen, 0)
    forward_all()
    gather_start(2)
    sent_all(g_copy)
    gather_pass()
    gather_finish()
    inc[...] = image[...]

    def step(it, carry):
        for h in range(2):
            for j in range(pairs):
                for v in range(n_vars):
                    rows = flat_rows(j, v)
                    misfit[h, rows, :] = jnp.clip(inc[h, rows, :] - obs[h, rows, :], -thr[v], thr[v])
        for bs in ((0,), (1,), (2, 3)):
            adjoint_first(bs)
        over_chunks(adjoint_second)

        def gradient(q):
            def body(b, squares):
                recv_both(c_copy, q, [b])
                rows = pl.ds(*groups[q])
                grad = w[b, rows, :] + own[b, rows, :] + part_recv[0, b, rows, :] + part_recv[1, b, rows, :]
                halo[1, b, rows, :] = grad
                send_both(g_copy, q, [b])
                return squares + total_of(grad * grad)

            return lax.fori_loop(0, blocks, body, jnp.zeros((8, LANES), jnp.float32))

        grad_sq = gradient(0)
        grad_sq = grad_sq + gradient(1)
        image_sq = forward_all()
        sums = jnp.concatenate([jnp.sum(grad_sq, axis=0, keepdims=True), jnp.sum(image_sq, axis=0, keepdims=True)], axis=0)
        lat_send[...] = sums
        for k in range(n_lat - 1):
            sl_copy(it, k).start()
        gather_start(2)
        sent_all(c_copy)
        sent_all(g_copy)
        gather_pass()
        for k in range(n_lat - 1):
            sl_copy(it, k).wait_recv()
        sums = sums + jnp.sum(lat_recv[it], axis=0)
        mem_send[...] = sums
        for k in range(n_mem - 1):
            sm_copy(it, k).start()
        for k in range(n_lat - 1):
            sl_copy(it, k).wait_send()
        gather_finish()
        for k in range(n_mem - 1):
            sm_copy(it, k).wait_recv()
        sums = sums + jnp.sum(mem_recv[it], axis=0)
        g2 = jnp.sum(sums[0:1, :], axis=1, keepdims=True)
        h2 = jnp.sum(sums[1:2, :], axis=1, keepdims=True)
        step_len = g2 / (g2 + h2)
        inc[...] = inc[...] - step_len[None] * image[...]
        for b in range(blocks):
            w[b] = w[b] - step_len * halo[1, b]
        for k in range(n_mem - 1):
            sm_copy(it, k).wait_send()
        return carry

    lax.fori_loop(0, STEPS, step, 0)

    for b in range(blocks):
        members = pl.ds(b * GROUP, GROUP)
        tail = w[b, tail_rows, :]
        weights_out[:, members, :LANES] = w[b, first_rows, :].reshape(n_rows, GROUP, LANES)
        weights_out[:, members, LANES:2 * LANES] = w[b, second_rows, :].reshape(n_rows, GROUP, LANES)
        weights_out[:n_rows // 2, members, 2 * LANES:] = tail[:, :LANES // 2].reshape(n_rows // 2, GROUP, LANES // 2)
        weights_out[n_rows // 2:, members, 2 * LANES:] = tail[:, LANES // 2:].reshape(n_rows // 2, GROUP, LANES // 2)

    share = inc_out.shape[2]
    first = mem * share // LANES
    shift = mem * share - first * LANES

    def lane_tile(t, v):
        j = jnp.where(t % 2 == 1, (t - 1) // 2, (t // 2 + pairs - 1) % pairs)
        row = jnp.int32(0)
        for i in range(pairs):
            row = jnp.where(j == i, starts[i] + v * fine, row)
        return inc[1 - t % 2, pl.ds(pl.multiple_of(row, 8), fine), :]

    fine_lane = lax.broadcasted_iota(jnp.int32, (fine, LANES), 1)
    for v in range(n_vars):
        a = pltpu.roll(lane_tile(first, v), (LANES - shift) % LANES, 1)
        b = pltpu.roll(lane_tile(first + 1, v), (LANES - shift) % LANES, 1)
        inc_out[v, :, :LANES] = jnp.where(fine_lane < LANES - shift, a, b)
        inc_out[v, :, LANES:] = b[:, :share - LANES]


def per_device(n_mem, n_lat, perturbations, control, innovations, thresholds):
    members, coarse_rows, coarse_cols = control.shape
    n_vars, fine_rows, fine_cols = innovations.shape
    blocks = members // GROUP
    seg = GROUP * coarse_rows
    packed = seg * coarse_cols // LANES
    n_z = n_mem // 2
    tile_rows = n_vars * fine_rows
    pairs = fine_cols // (2 * LANES)
    parts, bases, flat = [], [], 0
    starts = [0] * pairs
    for tiles in ((0, 4), (1, 2), (3,)):
        parts.append(-(-len(tiles) * tile_rows // n_z // 8) * 8)
        bases.append(flat)
        for i, j in enumerate(tiles):
            starts[j] = flat + i * tile_rows
        flat += n_z * parts[-1]
    vmem = pl.BlockSpec(memory_space=pltpu.VMEM)
    whole = pl.BlockSpec(memory_space=pl.ANY)
    f32 = jnp.float32
    bf16 = jnp.bfloat16
    dma = pltpu.SemaphoreType.DMA
    constants = tables(coarse_rows)
    ordered = control.transpose(1, 0, 2)
    shapes = (
        jax.ShapeDtypeStruct(ordered.shape, f32),
        jax.ShapeDtypeStruct((n_vars, fine_rows, fine_cols // n_mem), f32))
    weights, increment = pl.pallas_call(
        functools.partial(kernel, n_mem, n_lat, seg, (bases, parts, starts)),
        out_shape=tuple(pltpu.VMEM(x.shape, f32) for x in shapes),
        in_specs=[whole, whole, whole, pl.BlockSpec(memory_space=pltpu.SMEM)] + [whole] * 6,
        out_specs=(vmem, vmem),
        scratch_shapes=[
            pltpu.VMEM(perturbations.shape, bf16),
            pltpu.VMEM(perturbations.shape, f32),
            pltpu.VMEM(ordered.shape, f32),
            pltpu.VMEM(innovations.shape, f32),
            pltpu.VMEM(constants[0].shape[1:], bf16),
            pltpu.VMEM(constants[1].shape[1:], bf16),
            pltpu.VMEM(constants[2].shape, bf16),
            pltpu.VMEM(constants[3].shape, bf16),
            pltpu.VMEM(constants[4].shape, bf16),
            pltpu.VMEM(constants[5].shape, bf16),
            pltpu.VMEM((3, blocks, packed, LANES), f32),
            pltpu.VMEM((2, blocks, packed, LANES), f32),
            pltpu.VMEM((2, blocks, packed, LANES), f32),
            pltpu.VMEM((blocks, packed, LANES), f32),
            pltpu.VMEM((blocks, packed, LANES), f32),
            pltpu.VMEM((blocks, GROUP * fine_rows, LANES), f32),
            pltpu.VMEM((blocks, 2, GROUP * fine_rows, 2 * LANES), bf16),
            pltpu.VMEM((2, flat, LANES), f32),
            pltpu.VMEM((flat, LANES), f32),
            pltpu.VMEM((flat, LANES), f32),
            pltpu.VMEM((n_z - 1, sum(parts), LANES), f32),
            pltpu.VMEM((2, flat, LANES), f32),
            pltpu.VMEM((2, flat, LANES), f32),
            pltpu.VMEM((2, flat, LANES), f32),
            pltpu.VMEM((2, flat, LANES), f32),
            pltpu.VMEM((2, LANES), f32),
            pltpu.VMEM((STEPS, n_lat - 1, 2, LANES), f32),
            pltpu.VMEM((2, LANES), f32),
            pltpu.VMEM((STEPS, n_mem - 1, 2, LANES), f32),
            dma((blocks,)), dma((8,)),
            dma((2, 2, blocks)), dma((2, 2, blocks)), dma((2, 2, blocks)), dma((2, 2, blocks)),
            dma((3,)), dma((3,)), dma((3, n_z - 1)), dma((3, n_z - 1)), dma((3, n_z - 1)), dma((3, n_z - 1)), dma((1,)), dma((1,)),
            dma((STEPS, n_lat - 1)), dma((STEPS, n_lat - 1)), dma((STEPS, n_mem - 1)), dma((STEPS, n_mem - 1)),
        ],
        compiler_params=pltpu.CompilerParams(collective_id=0, has_side_effects=True),
    )(perturbations, ordered, innovations, thresholds, *constants)
    return weights.transpose(1, 0, 2), increment


def solution(mesh):
    return jax.shard_map(
        functools.partial(per_device, mesh.shape["mem"], mesh.shape["lat"]),
        mesh=mesh,
        in_specs=(P("mem", None, "lat", None), P("mem", "lat", None), P(None, "lat", None), P()),
        out_specs=(P("mem", "lat", None), P(None, "lat", "mem")),
        check_vma=False,
    )
```

```python
import functools

import jax
import jax.numpy as jnp
import numpy as np
from jax import lax
from jax.experimental import pallas as pl
from jax.experimental.pallas import tpu as pltpu
from jax.sharding import PartitionSpec as P

RATIO = 4
HALF = 5
STEPS = 2
SIDE = 4
GROUP = 8
PAIR = 2
LANES = 128
MESH = pl.DeviceIdType.MESH
SCALE = 96.0


def tent(distance):
    return np.maximum(0.0, 1.0 - np.abs(distance) / RATIO)


def row_operator(coarse_rows, first, last):
    fine = np.arange(RATIO * coarse_rows)[:, None]
    inner = np.arange(-1, coarse_rows + 1)
    up = tent(fine + 0.5 - RATIO * inner[None, :] - RATIO / 2)
    if first:
        up[:, 0] = 0.0
    if last:
        up[:, -1] = 0.0
    outer = np.arange(-coarse_rows, 2 * coarse_rows)
    gap = np.abs(inner[:, None] - outer[None, :])
    smooth = np.where(gap <= HALF, (1.0 - gap / (HALF + 1)) / 2, 0.0)
    return np.rint(SCALE * up @ smooth)


def block_rows(operator):
    fine, wide = operator.shape
    out = np.zeros((GROUP, fine, wide, GROUP))
    for member in range(GROUP):
        out[member, :, :, member] = operator
    return out.reshape(GROUP * fine, wide * GROUP)


def tables(coarse_rows):
    ops = [block_rows(row_operator(coarse_rows, *ends)) for ends in ((True, False), (False, False), (False, True))]
    rows_up = np.stack(ops)
    rows_down = np.stack([op.T for op in ops])
    fine = np.arange(2 * LANES)[None, :]
    narrow = tent(LANES + fine + 0.5 - RATIO * np.arange(LANES)[:, None] - RATIO / 2)
    wide = tent(3 * LANES + fine + 0.5 - RATIO * np.arange(2 * LANES)[:, None] - RATIO / 2)
    narrow_up = np.concatenate([narrow, narrow], 0)
    wide_up = np.concatenate([wide[:LANES], wide[:LANES], wide[LANES:], wide[LANES:]], 0)
    narrow_down = np.concatenate([narrow.T, narrow.T], 0)
    wide_down = np.concatenate([wide.T, wide.T], 0)
    return [jnp.asarray(t, jnp.bfloat16) for t in (rows_up, rows_down, narrow_up, wide_up, narrow_down, wide_down)]


def split(x):
    high = x.astype(jnp.bfloat16)
    return high, (x - high.astype(jnp.float32)).astype(jnp.bfloat16)


def dot(a, b):
    return jnp.dot(a, b, preferred_element_type=jnp.float32)


def kernel(
    n_mem, n_lat, seg, layout,
    pert_hbm, control_hbm, innov_hbm, thr_hbm, rows_up_hbm, rows_down_hbm, narrow_up_hbm, wide_up_hbm, narrow_down_hbm, wide_down_hbm,
    weights_out, inc_out,
    thr, pert_raw, pert, control, innov, rows_up, rows_down, narrow_up, wide_up, narrow_down, wide_down,
    halo, part_send, part_recv, own, w, spare, lifted, acc, pair_recv, half_sum, z_recv, image, inc, misfit, obs,
    lat_send, lat_recv, mem_send, mem_recv,
    pert_sem, load_sem, g_send, g_recv, c_send, c_recv, p_ss, p_rs, z_ss, z_rs, ag_ss, ag_rs, im_ss, im_rs, sl_ss, sl_rs, sm_ss, sm_rs,
):
    mem = lax.axis_index("mem")
    lat = lax.axis_index("lat")
    core = lax.rem(mem, 2)
    n_z = n_mem // 2
    z = mem // 2
    blocks = pert.shape[0] // GROUP
    chunks = blocks // PAIR
    n_vars = pert.shape[1]
    fine = pert.shape[2]
    tiles = pert.shape[3] // LANES
    pairs = tiles // 2
    tile_rows = n_vars * fine
    half = seg // 2
    n_rows = seg // GROUP
    case = jnp.where(lat == 0, 0, jnp.where(lat == n_lat - 1, 2, 1))
    up_id = (mem, jnp.maximum(lat - 1, 0))
    down_id = (mem, jnp.minimum(lat + 1, n_lat - 1))
    has_up = lat > 0
    has_down = lat < n_lat - 1
    partner = (2 * z + 1 - core, lat)
    z_peers = [(2 * lax.rem(z + k, n_z) + core, lat) for k in range(1, n_z)]
    mem_peers = [(2 * lax.rem(z + k, n_z) + c, lat) for k in (2, 1, 3) for c in (core, 1 - core)] + [partner]
    far = sorted(((i, k) for i in range(SIDE) for k in range(SIDE) if i or k), key=lambda at: -sum(min(d, SIDE - d) for d in at))
    lat_peers = [(mem, lax.rem(lat // SIDE + i, SIDE) * SIDE + lax.rem(lat + k, SIDE)) for i, k in far]
    groups = ((0, seg + half), (seg + half, seg))
    first_rows, tail_rows, second_rows = pl.ds(0, seg), pl.ds(seg, half), pl.ds(seg + half, seg)
    bases, parts, starts = layout
    z_bases = [sum(parts[:i]) for i in range(3)]

    loads = [
        (control_hbm, control), (rows_up_hbm.at[case], rows_up), (narrow_up_hbm, narrow_up), (wide_up_hbm, wide_up),
        (innov_hbm, innov), (rows_down_hbm.at[case], rows_down), (narrow_down_hbm, narrow_down), (wide_down_hbm, wide_down),
        (thr_hbm, thr),
    ]
    loads = [pltpu.make_async_copy(src, dst, load_sem.at[i]) for i, (src, dst) in enumerate(loads)]

    loads[0].start()
    barrier = pltpu.get_barrier_semaphore()
    for peer in lat_peers + mem_peers:
        pl.semaphore_signal(barrier, inc=1, device_id=peer, device_id_type=MESH)

    def pert_copy(c):
        rows = pl.ds(c * GROUP, GROUP)
        return pltpu.make_async_copy(pert_hbm.at[rows], pert_raw.at[rows], pert_sem.at[c])

    for load in loads[1:4]:
        load.start()
    for c in range(blocks):
        pert_copy(c).start()
    for load in loads[4:]:
        load.start()

    lane = lax.broadcasted_iota(jnp.int32, (half, LANES), 1)
    left = lane < LANES // 2

    def swap(x):
        return pltpu.roll(x, LANES // 2, 1)

    def g_copy(q, b, up):
        rows = pl.ds(*groups[q])
        i = 0 if up else 1
        return pltpu.make_async_remote_copy(
            src_ref=halo.at[1, b, rows], dst_ref=halo.at[2 if up else 0, b, rows],
            send_sem=g_send.at[i, q, b], recv_sem=g_recv.at[i, q, b],
            device_id=up_id if up else down_id, device_id_type=MESH)

    def c_copy(q, b, up):
        rows = pl.ds(*groups[q])
        i = 0 if up else 1
        return pltpu.make_async_remote_copy(
            src_ref=part_send.at[i, b, rows], dst_ref=part_recv.at[i, b, rows],
            send_sem=c_send.at[i, q, b], recv_sem=c_recv.at[i, q, b],
            device_id=up_id if up else down_id, device_id_type=MESH)

    def send_both(copy, q, bs):
        @pl.when(has_up)
        def _():
            for b in bs:
                copy(q, b, True).start()

        @pl.when(has_down)
        def _():
            for b in bs:
                copy(q, b, False).start()

    def recv_both(copy, q, bs):
        @pl.when(has_down)
        def _():
            for b in bs:
                copy(q, b, True).wait_recv()

        @pl.when(has_up)
        def _():
            for b in bs:
                copy(q, b, False).wait_recv()

    def sent_all(copy):
        def body(b, carry):
            for q in range(2):
                @pl.when(has_up)
                def _():
                    copy(q, b, True).wait_send()

                @pl.when(has_down)
                def _():
                    copy(q, b, False).wait_send()
            return carry

        lax.fori_loop(0, blocks, body, 0)

    def over_chunks(f):
        def body(c, carry):
            f([c * PAIR + i for i in range(PAIR)])
            return carry

        lax.fori_loop(0, chunks, body, 0)

    def lane_pair(j):
        return 2 * j + 1, (2 * j + 2) % tiles

    def flat_rows(j, v):
        return pl.ds(starts[j] + v * fine, fine)

    def both_pieces(x):
        high, low = split(x)
        return jnp.concatenate([high, low], axis=1)

    def lift(g, b):
        pieces = []
        for i in range(3):
            if g < 2:
                pieces.append(halo[i, b, second_rows if g else first_rows, :])
            else:
                first = halo[i, b, first_rows, :]
                tail = halo[i, b, tail_rows, :]
                pieces.append(jnp.where(left, tail, swap(first[:half])))
                pieces.append(jnp.where(left, swap(tail), swap(first[half:])))
        wide = dot(rows_up[...], both_pieces(jnp.concatenate(pieces, axis=0)))
        return both_pieces(wide[:, :LANES] + wide[:, LANES:])

    def accumulate(j, bs, fields):
        for h, t in enumerate(lane_pair(j)):
            for v in range(n_vars):
                total = acc[h, flat_rows(j, v), :]
                for b, field in zip(bs, fields):
                    f = field[:, h * LANES:(h + 1) * LANES].reshape(GROUP, fine, LANES)
                    p = pert[pl.ds(b * GROUP, GROUP), v, :, t * LANES:(t + 1) * LANES]
                    total = total + jnp.sum(p * f, axis=0)
                acc[h, flat_rows(j, v), :] = total

    def forward_first(bs):
        recv_both(g_copy, 0, bs)
        zero_th = [lift(0, b) for b in bs]
        two = [lift(2, b) for b in bs]
        for b, p, q in zip(bs, zero_th, two):
            lifted[b, 0] = p
            lifted[b, 1] = q
        accumulate(0, bs, [dot(value, narrow_up[...]) for value in zero_th])
        accumulate(4, bs, [dot(value, narrow_up[...]) for value in two])

    def odd_tile(a, b):
        return dot(a, wide_up[:2 * LANES, :]) + dot(b, wide_up[2 * LANES:, :])

    def forward_second(b, split_at=None):
        recv_both(g_copy, 1, [b])
        one = lift(1, b)
        accumulate(1, [b], [odd_tile(lifted[b, 0], one)])
        accumulate(2, [b], [dot(one, narrow_up[...])])
        if split_at is not None:
            split_at()
        accumulate(3, [b], [odd_tile(one, lifted[b, 1])])

    def weighted(j, b):
        pieces = []
        for h, t in enumerate(lane_pair(j)):
            total = None
            for v in range(n_vars):
                p = pert[pl.ds(b * GROUP, GROUP), v, :, t * LANES:(t + 1) * LANES]
                term = p * misfit[h, flat_rows(j, v), :][None]
                total = term if total is None else total + term
            pieces.append(split(total.reshape(GROUP * fine, LANES)))
        lhs = jnp.concatenate([pieces[0][0], pieces[1][0], pieces[0][1], pieces[1][1]], axis=1)
        return dot(lhs, narrow_down[...] if j % 2 == 0 else wide_down[...])

    def lower(x):
        wide = dot(rows_down[...], both_pieces(x))
        return (wide[:, :LANES] + wide[:, LANES:]) * (1.0 / SCALE)

    def keep(b, rows, coarse):
        part_send[0, b, rows, :] = coarse[0]
        own[b, rows, :] = coarse[1]
        part_send[1, b, rows, :] = coarse[2]

    def three(x):
        return x[:seg], x[seg:2 * seg], x[2 * seg:]

    def adjoint_first(bs):
        for b in bs:
            last = weighted(4, b)
            wide = weighted(1, b)
            high = weighted(3, b)
            wrapped = jnp.where(lax.broadcasted_iota(jnp.int32, last.shape, 1) < LANES // 2, swap(last), 0.0)
            first = weighted(0, b) + wide[:, :LANES] + wrapped
            spare[b] = wide[:, LANES:] + high[:, :LANES]
            keep(b, first_rows, three(lower(first)))
            ends = three(lower(last + high[:, LANES:]))
            keep(b, tail_rows, [jnp.where(left, e[:half], swap(e[half:])) for e in ends])
        send_both(c_copy, 0, bs)

    def adjoint_second(bs):
        for b in bs:
            keep(b, second_rows, three(lower(spare[b] + weighted(2, b))))
        send_both(c_copy, 1, bs)

    def region(s):
        return pl.ds(bases[s], n_z * parts[s])

    def part_rows(s, at):
        return pl.ds(pl.multiple_of(bases[s] + at * parts[s], 8), parts[s])

    def pair_copy(s):
        return pltpu.make_async_remote_copy(
            src_ref=acc.at[1 - core, region(s)], dst_ref=pair_recv.at[region(s)],
            send_sem=p_ss.at[s], recv_sem=p_rs.at[s], device_id=partner, device_id_type=MESH)

    def z_copy(s, k):
        return pltpu.make_async_remote_copy(
            src_ref=half_sum.at[part_rows(s, lax.rem(z + k + 1, n_z))], dst_ref=z_recv.at[k, pl.ds(z_bases[s], parts[s])],
            send_sem=z_ss.at[s, k], recv_sem=z_rs.at[s, k], device_id=z_peers[k], device_id_type=MESH)

    def ag_copy(s, k, source):
        return pltpu.make_async_remote_copy(
            src_ref=image.at[core, part_rows(s, source)], dst_ref=image.at[core, part_rows(s, source)],
            send_sem=ag_ss.at[s, k], recv_sem=ag_rs.at[s, k], device_id=z_peers[k], device_id_type=MESH)

    def image_copy(index):
        return pltpu.make_async_remote_copy(
            src_ref=image.at[index], dst_ref=image.at[index],
            send_sem=im_ss.at[0], recv_sem=im_rs.at[0], device_id=partner, device_id_type=MESH)

    def pair_finish(s):
        pair_copy(s).wait_recv()
        half_sum[region(s), :] = acc[core, region(s), :] + pair_recv[region(s), :]
        for k in range(n_z - 1):
            z_copy(s, k).start()

    def z_finish(s):
        for k in range(n_z - 1):
            z_copy(s, k).wait_recv()
        total = half_sum[part_rows(s, z), :]
        for k in range(n_z - 1):
            total = total + z_recv[k, pl.ds(z_bases[s], parts[s]), :]
        total = total * (1.0 / SCALE)
        image[core, part_rows(s, z), :] = total
        if s < 2:
            gather_start(s)
        return total_of(total * total)

    def gather_start(s):
        for k in range(n_z - 1):
            ag_copy(s, k, z).start()

    def gather_pass():
        for s in range(3):
            for k in range(n_z - 1):
                ag_copy(s, k, lax.rem(z + n_z - 1 - k, n_z)).wait_recv()
        image_copy(core).start()

    def gather_finish():
        image_copy(1 - core).wait_recv()
        image_copy(core).wait_send()
        for s in range(3):
            pair_copy(s).wait_send()
            for k in range(n_z - 1):
                z_copy(s, k).wait_send()
                ag_copy(s, k, z).wait_send()

    def total_of(squares):
        return jnp.sum(squares.reshape(-1, 8, LANES), axis=0)

    def forward_all():
        acc[...] = jnp.zeros_like(acc)
        over_chunks(forward_first)
        pair_copy(0).start()

        def body(b, carry):
            forward_second(b)
            return carry

        lax.fori_loop(0, blocks - 1, body, 0)
        pair_finish(0)
        forward_second(blocks - 1, lambda: pair_copy(1).start())
        pair_copy(2).start()
        pair_finish(1)
        pair_finish(2)
        squares = z_finish(0)
        squares = squares + z_finish(1)
        squares = squares + z_finish(2)
        return squares

    def sl_copy(it, k):
        return pltpu.make_async_remote_copy(
            src_ref=lat_send, dst_ref=lat_recv.at[it, k],
            send_sem=sl_ss.at[it, k], recv_sem=sl_rs.at[it, k], device_id=lat_peers[k], device_id_type=MESH)

    def sm_copy(it, k):
        return pltpu.make_async_remote_copy(
            src_ref=mem_send, dst_ref=mem_recv.at[it, k],
            send_sem=sm_ss.at[it, k], recv_sem=sm_rs.at[it, k], device_id=mem_peers[k], device_id_type=MESH)

    loads[0].wait()
    for b in range(blocks):
        block = control[:, pl.ds(b * GROUP, GROUP), :].reshape(seg, control.shape[2])
        ends = block[:, 2 * LANES:]
        tail = jnp.concatenate([ends[:half], ends[half:]], axis=1)
        for rows, value in ((first_rows, block[:, :LANES]), (second_rows, block[:, LANES:2 * LANES]), (tail_rows, tail)):
            halo[1, b, rows, :] = value
            w[b, rows, :] = value

    pl.semaphore_wait(barrier, len(lat_peers) + len(mem_peers))
    over_chunks(functools.partial(send_both, g_copy, 0))
    over_chunks(functools.partial(send_both, g_copy, 1))

    zero = jnp.zeros(halo.shape[2:], jnp.float32)

    @pl.when(jnp.logical_not(has_up))
    def _():
        for b in range(blocks):
            halo[0, b] = zero
            part_recv[1, b] = zero

    @pl.when(jnp.logical_not(has_down))
    def _():
        for b in range(blocks):
            halo[2, b] = zero
            part_recv[0, b] = zero

    for load in loads[1:]:
        load.wait()
    for j in range(pairs):
        for h, t in enumerate(lane_pair(j)):
            for v in range(n_vars):
                obs[h, flat_rows(j, v), :] = innov[v, :, t * LANES:(t + 1) * LANES]
    for c in range(blocks):
        pert_copy(c).wait()

    def widen(m, carry):
        pert[m] = pert_raw[m].astype(jnp.float32)
        return carry

    lax.fori_loop(0, pert.shape[0], widen, 0)
    forward_all()
    gather_start(2)
    sent_all(g_copy)
    gather_pass()
    gather_finish()
    inc[...] = image[...]

    def step(it, step_len):
        for h in range(2):
            for j in (4, 0, 1, 3, 2):
                for v in range(n_vars):
                    rows = flat_rows(j, v)
                    moved = inc[h, rows, :] - step_len * image[h, rows, :]
                    inc[h, rows, :] = moved
                    misfit[h, rows, :] = jnp.clip(moved - obs[h, rows, :], -thr[v], thr[v])
        for bs in ((0,), (1,), (2, 3)):
            adjoint_first(bs)
        over_chunks(adjoint_second)
        for b in range(blocks):
            w[b] = w[b] - step_len * halo[1, b]

        def gradient(q):
            def body(b, squares):
                recv_both(c_copy, q, [b])
                rows = pl.ds(*groups[q])
                grad = w[b, rows, :] + own[b, rows, :] + part_recv[0, b, rows, :] + part_recv[1, b, rows, :]
                halo[1, b, rows, :] = grad
                send_both(g_copy, q, [b])
                return squares + total_of(grad * grad)

            return lax.fori_loop(0, blocks, body, jnp.zeros((8, LANES), jnp.float32))

        grad_sq = gradient(0)
        grad_sq = grad_sq + gradient(1)
        image_sq = forward_all()
        sums = jnp.concatenate([jnp.sum(grad_sq, axis=0, keepdims=True), jnp.sum(image_sq, axis=0, keepdims=True)], axis=0)
        mem_send[...] = sums
        for k in range(n_mem - 1):
            sm_copy(it, k).start()
        gather_start(2)
        sent_all(c_copy)
        sent_all(g_copy)
        for k in range(n_mem - 1):
            sm_copy(it, k).wait_recv()
        sums = sums + jnp.sum(mem_recv[it], axis=0)
        lat_send[...] = sums
        for k in range(n_lat - 1):
            sl_copy(it, k).start()
        gather_pass()
        gather_finish()
        for k in range(n_lat - 1):
            sl_copy(it, k).wait_recv()
        sums = sums + jnp.sum(lat_recv[it], axis=0)
        for k in range(n_lat - 1):
            sl_copy(it, k).wait_send()
        g2 = jnp.sum(sums[0:1, :], axis=1, keepdims=True)
        h2 = jnp.sum(sums[1:2, :], axis=1, keepdims=True)
        step_len = g2 / (g2 + h2)
        for k in range(n_mem - 1):
            sm_copy(it, k).wait_send()
        return step_len

    step_len = lax.fori_loop(0, STEPS, step, jnp.zeros((1, 1), jnp.float32))

    for b in range(blocks):
        members = pl.ds(b * GROUP, GROUP)
        final = w[b] - step_len * halo[1, b]
        one, tail, two = final[:seg], final[seg:seg + half], final[seg + half:]
        weights_out[:, members, :LANES] = one.reshape(n_rows, GROUP, LANES)
        weights_out[:, members, LANES:2 * LANES] = two.reshape(n_rows, GROUP, LANES)
        weights_out[:n_rows // 2, members, 2 * LANES:] = tail[:, :LANES // 2].reshape(n_rows // 2, GROUP, LANES // 2)
        weights_out[n_rows // 2:, members, 2 * LANES:] = tail[:, LANES // 2:].reshape(n_rows // 2, GROUP, LANES // 2)

    share = inc_out.shape[2]
    first = mem * share // LANES
    shift = mem * share - first * LANES

    def lane_tile(t, v):
        j = jnp.where(t % 2 == 1, (t - 1) // 2, (t // 2 + pairs - 1) % pairs)
        row = jnp.int32(0)
        for i in range(pairs):
            row = jnp.where(j == i, starts[i] + v * fine, row)
        rows = pl.ds(pl.multiple_of(row, 8), fine)
        return inc[1 - t % 2, rows, :] - step_len * image[1 - t % 2, rows, :]

    fine_lane = lax.broadcasted_iota(jnp.int32, (fine, LANES), 1)
    for v in range(n_vars):
        a = pltpu.roll(lane_tile(first, v), (LANES - shift) % LANES, 1)
        b = pltpu.roll(lane_tile(first + 1, v), (LANES - shift) % LANES, 1)
        inc_out[v, :, :LANES] = jnp.where(fine_lane < LANES - shift, a, b)
        inc_out[v, :, LANES:] = b[:, :share - LANES]


def per_device(n_mem, n_lat, perturbations, control, innovations, thresholds):
    members, coarse_rows, coarse_cols = control.shape
    n_vars, fine_rows, fine_cols = innovations.shape
    blocks = members // GROUP
    seg = GROUP * coarse_rows
    packed = seg * coarse_cols // LANES
    n_z = n_mem // 2
    tile_rows = n_vars * fine_rows
    pairs = fine_cols // (2 * LANES)
    parts, bases, flat = [], [], 0
    starts = [0] * pairs
    for tiles in ((0, 4), (1, 2), (3,)):
        parts.append(-(-len(tiles) * tile_rows // n_z // 8) * 8)
        bases.append(flat)
        for i, j in enumerate(tiles):
            starts[j] = flat + i * tile_rows
        flat += n_z * parts[-1]
    vmem = pl.BlockSpec(memory_space=pltpu.VMEM)
    whole = pl.BlockSpec(memory_space=pl.ANY)
    f32 = jnp.float32
    bf16 = jnp.bfloat16
    dma = pltpu.SemaphoreType.DMA
    constants = tables(coarse_rows)
    ordered = control.transpose(1, 0, 2)
    shapes = (
        jax.ShapeDtypeStruct(ordered.shape, f32),
        jax.ShapeDtypeStruct((n_vars, fine_rows, fine_cols // n_mem), f32))
    weights, increment = pl.pallas_call(
        functools.partial(kernel, n_mem, n_lat, seg, (bases, parts, starts)),
        out_shape=tuple(pltpu.VMEM(x.shape, f32) for x in shapes),
        in_specs=[whole] * 10,
        out_specs=(vmem, vmem),
        scratch_shapes=[
            pltpu.SMEM(thresholds.shape, f32),
            pltpu.VMEM(perturbations.shape, bf16),
            pltpu.VMEM(perturbations.shape, f32),
            pltpu.VMEM(ordered.shape, f32),
            pltpu.VMEM(innovations.shape, f32),
            pltpu.VMEM(constants[0].shape[1:], bf16),
            pltpu.VMEM(constants[1].shape[1:], bf16),
            pltpu.VMEM(constants[2].shape, bf16),
            pltpu.VMEM(constants[3].shape, bf16),
            pltpu.VMEM(constants[4].shape, bf16),
            pltpu.VMEM(constants[5].shape, bf16),
            pltpu.VMEM((3, blocks, packed, LANES), f32),
            pltpu.VMEM((2, blocks, packed, LANES), f32),
            pltpu.VMEM((2, blocks, packed, LANES), f32),
            pltpu.VMEM((blocks, packed, LANES), f32),
            pltpu.VMEM((blocks, packed, LANES), f32),
            pltpu.VMEM((blocks, GROUP * fine_rows, LANES), f32),
            pltpu.VMEM((blocks, 2, GROUP * fine_rows, 2 * LANES), bf16),
            pltpu.VMEM((2, flat, LANES), f32),
            pltpu.VMEM((flat, LANES), f32),
            pltpu.VMEM((flat, LANES), f32),
            pltpu.VMEM((n_z - 1, sum(parts), LANES), f32),
            pltpu.VMEM((2, flat, LANES), f32),
            pltpu.VMEM((2, flat, LANES), f32),
            pltpu.VMEM((2, flat, LANES), f32),
            pltpu.VMEM((2, flat, LANES), f32),
            pltpu.VMEM((2, LANES), f32),
            pltpu.VMEM((STEPS, n_lat - 1, 2, LANES), f32),
            pltpu.VMEM((2, LANES), f32),
            pltpu.VMEM((STEPS, n_mem - 1, 2, LANES), f32),
            dma((blocks,)), dma((9,)),
            dma((2, 2, blocks)), dma((2, 2, blocks)), dma((2, 2, blocks)), dma((2, 2, blocks)),
            dma((3,)), dma((3,)), dma((3, n_z - 1)), dma((3, n_z - 1)), dma((3, n_z - 1)), dma((3, n_z - 1)), dma((1,)), dma((1,)),
            dma((STEPS, n_lat - 1)), dma((STEPS, n_lat - 1)), dma((STEPS, n_mem - 1)), dma((STEPS, n_mem - 1)),
        ],
        compiler_params=pltpu.CompilerParams(collective_id=0, has_side_effects=True),
    )(perturbations, ordered, innovations, thresholds, *constants)
    return weights.transpose(1, 0, 2), increment


def solution(mesh):
    return jax.shard_map(
        functools.partial(per_device, mesh.shape["mem"], mesh.shape["lat"]),
        mesh=mesh,
        in_specs=(P("mem", None, "lat", None), P("mem", "lat", None), P(None, "lat", None), P()),
        out_specs=(P("mem", "lat", None), P(None, "lat", "mem")),
        check_vma=False,
    )
```

```python
import functools

import jax
import jax.numpy as jnp
import numpy as np
from jax import lax
from jax.experimental import pallas as pl
from jax.experimental.pallas import tpu as pltpu
from jax.sharding import PartitionSpec as P

RATIO = 4
HALF = 5
STEPS = 2
SIDE = 4
GROUP = 8
PAIR = 2
LANES = 128
MESH = pl.DeviceIdType.MESH
SCALE = 96.0


def tent(distance):
    return np.maximum(0.0, 1.0 - np.abs(distance) / RATIO)


def row_operator(coarse_rows, first, last):
    fine = np.arange(RATIO * coarse_rows)[:, None]
    inner = np.arange(-1, coarse_rows + 1)
    up = tent(fine + 0.5 - RATIO * inner[None, :] - RATIO / 2)
    if first:
        up[:, 0] = 0.0
    if last:
        up[:, -1] = 0.0
    outer = np.arange(-coarse_rows, 2 * coarse_rows)
    gap = np.abs(inner[:, None] - outer[None, :])
    smooth = np.where(gap <= HALF, (1.0 - gap / (HALF + 1)) / 2, 0.0)
    return np.rint(SCALE * up @ smooth)


def block_rows(operator):
    fine, wide = operator.shape
    out = np.zeros((GROUP, fine, wide, GROUP))
    for member in range(GROUP):
        out[member, :, :, member] = operator
    return out.reshape(GROUP * fine, wide * GROUP)


def tables(coarse_rows):
    ops = [block_rows(row_operator(coarse_rows, *ends)) for ends in ((True, False), (False, False), (False, True))]
    rows_up = np.stack(ops)
    rows_down = np.stack([op.T for op in ops])
    fine = np.arange(2 * LANES)[None, :]
    narrow = tent(LANES + fine + 0.5 - RATIO * np.arange(LANES)[:, None] - RATIO / 2)
    wide = tent(3 * LANES + fine + 0.5 - RATIO * np.arange(2 * LANES)[:, None] - RATIO / 2)
    narrow_up = np.concatenate([narrow, narrow], 0)
    wide_up = np.concatenate([wide[:LANES], wide[:LANES], wide[LANES:], wide[LANES:]], 0)
    narrow_down = np.concatenate([narrow.T, narrow.T], 0)
    wide_down = np.concatenate([wide.T, wide.T], 0)
    return [jnp.asarray(t, jnp.bfloat16) for t in (rows_up, rows_down, narrow_up, wide_up, narrow_down, wide_down)]


def split(x):
    high = x.astype(jnp.bfloat16)
    return high, (x - high.astype(jnp.float32)).astype(jnp.bfloat16)


def dot(a, b):
    return jnp.dot(a, b, preferred_element_type=jnp.float32)


def kernel(
    n_mem, n_lat, seg, layout,
    pert_hbm, control_hbm, innov_hbm, thr_hbm, rows_up_hbm, rows_down_hbm, narrow_up_hbm, wide_up_hbm, narrow_down_hbm, wide_down_hbm,
    weights_out, inc_out,
    thr, pert_raw, pert, control, innov, rows_up, rows_down, narrow_up, wide_up, narrow_down, wide_down,
    halo, part_send, part_recv, own, w, spare, lifted, acc, pair_recv, half_sum, z_recv, image, inc, misfit, obs,
    lat_send, lat_recv, mem_send, mem_recv,
    pert_sem, load_sem, g_send, g_recv, c_send, c_recv, p_ss, p_rs, z_ss, z_rs, ag_ss, ag_rs, im_ss, im_rs, sl_ss, sl_rs, sm_ss, sm_rs,
):
    mem = lax.axis_index("mem")
    lat = lax.axis_index("lat")
    core = lax.rem(mem, 2)
    n_z = n_mem // 2
    z = mem // 2
    blocks = pert.shape[0] // GROUP
    chunks = blocks // PAIR
    n_vars = pert.shape[1]
    fine = pert.shape[2]
    tiles = pert.shape[3] // LANES
    pairs = tiles // 2
    tile_rows = n_vars * fine
    half = seg // 2
    n_rows = seg // GROUP
    case = jnp.where(lat == 0, 0, jnp.where(lat == n_lat - 1, 2, 1))
    up_id = (mem, jnp.maximum(lat - 1, 0))
    down_id = (mem, jnp.minimum(lat + 1, n_lat - 1))
    has_up = lat > 0
    has_down = lat < n_lat - 1
    partner = (2 * z + 1 - core, lat)
    z_peers = [(2 * lax.rem(z + k, n_z) + core, lat) for k in range(1, n_z)]
    mem_peers = [(2 * lax.rem(z + k, n_z) + c, lat) for k in (2, 1, 3) for c in (core, 1 - core)] + [partner]
    far = sorted(((i, k) for i in range(SIDE) for k in range(SIDE) if i or k), key=lambda at: -sum(min(d, SIDE - d) for d in at))
    lat_peers = [(mem, lax.rem(lat // SIDE + i, SIDE) * SIDE + lax.rem(lat + k, SIDE)) for i, k in far]
    groups = ((0, seg + half), (seg + half, seg))
    first_rows, tail_rows, second_rows = pl.ds(0, seg), pl.ds(seg, half), pl.ds(seg + half, seg)
    bases, parts, starts = layout
    z_bases = [sum(parts[:i]) for i in range(3)]

    loads = [
        (control_hbm, control), (rows_up_hbm.at[case], rows_up), (narrow_up_hbm, narrow_up), (wide_up_hbm, wide_up),
        (innov_hbm, innov), (rows_down_hbm.at[case], rows_down), (narrow_down_hbm, narrow_down), (wide_down_hbm, wide_down),
        (thr_hbm, thr),
    ]
    loads = [pltpu.make_async_copy(src, dst, load_sem.at[i]) for i, (src, dst) in enumerate(loads)]

    loads[0].start()
    barrier = pltpu.get_barrier_semaphore()
    for peer in lat_peers + mem_peers:
        pl.semaphore_signal(barrier, inc=1, device_id=peer, device_id_type=MESH)

    def pert_copy(c):
        rows = pl.ds(c * GROUP, GROUP)
        return pltpu.make_async_copy(pert_hbm.at[rows], pert_raw.at[rows], pert_sem.at[c])

    for load in loads[1:4]:
        load.start()
    for c in range(blocks):
        pert_copy(c).start()
    for load in loads[4:]:
        load.start()

    lane = lax.broadcasted_iota(jnp.int32, (half, LANES), 1)
    left = lane < LANES // 2

    def swap(x):
        return pltpu.roll(x, LANES // 2, 1)

    def g_copy(q, b, up):
        rows = pl.ds(*groups[q])
        i = 0 if up else 1
        return pltpu.make_async_remote_copy(
            src_ref=halo.at[1, b, rows], dst_ref=halo.at[2 if up else 0, b, rows],
            send_sem=g_send.at[i, q, b], recv_sem=g_recv.at[i, q, b],
            device_id=up_id if up else down_id, device_id_type=MESH)

    def c_copy(q, b, up):
        rows = pl.ds(*groups[q])
        i = 0 if up else 1
        return pltpu.make_async_remote_copy(
            src_ref=part_send.at[i, b, rows], dst_ref=part_recv.at[i, b, rows],
            send_sem=c_send.at[i, q, b], recv_sem=c_recv.at[i, q, b],
            device_id=up_id if up else down_id, device_id_type=MESH)

    def send_both(copy, q, bs):
        @pl.when(has_up)
        def _():
            for b in bs:
                copy(q, b, True).start()

        @pl.when(has_down)
        def _():
            for b in bs:
                copy(q, b, False).start()

    def recv_both(copy, q, bs):
        @pl.when(has_down)
        def _():
            for b in bs:
                copy(q, b, True).wait_recv()

        @pl.when(has_up)
        def _():
            for b in bs:
                copy(q, b, False).wait_recv()

    def sent_all(copy):
        def body(b, carry):
            for q in range(2):
                @pl.when(has_up)
                def _():
                    copy(q, b, True).wait_send()

                @pl.when(has_down)
                def _():
                    copy(q, b, False).wait_send()
            return carry

        lax.fori_loop(0, blocks, body, 0)

    def over_chunks(f):
        def body(c, carry):
            f([c * PAIR + i for i in range(PAIR)])
            return carry

        lax.fori_loop(0, chunks, body, 0)

    def lane_pair(j):
        return 2 * j + 1, (2 * j + 2) % tiles

    def flat_rows(j, v):
        return pl.ds(starts[j] + v * fine, fine)

    def both_pieces(x):
        high, low = split(x)
        return jnp.concatenate([high, low], axis=1)

    def lift(g, b):
        pieces = []
        for i in range(3):
            if g < 2:
                pieces.append(halo[i, b, second_rows if g else first_rows, :])
            else:
                first = halo[i, b, first_rows, :]
                tail = halo[i, b, tail_rows, :]
                pieces.append(jnp.where(left, tail, swap(first[:half])))
                pieces.append(jnp.where(left, swap(tail), swap(first[half:])))
        wide = dot(rows_up[...], both_pieces(jnp.concatenate(pieces, axis=0)))
        return both_pieces(wide[:, :LANES] + wide[:, LANES:])

    def accumulate(j, bs, fields):
        for h, t in enumerate(lane_pair(j)):
            for v in range(n_vars):
                total = acc[h, flat_rows(j, v), :]
                for b, field in zip(bs, fields):
                    f = field[:, h * LANES:(h + 1) * LANES].reshape(GROUP, fine, LANES)
                    p = pert[pl.ds(b * GROUP, GROUP), v, :, t * LANES:(t + 1) * LANES]
                    total = total + jnp.sum(p * f, axis=0)
                acc[h, flat_rows(j, v), :] = total

    def forward_first(bs):
        recv_both(g_copy, 0, bs)
        zero_th = [lift(0, b) for b in bs]
        two = [lift(2, b) for b in bs]
        for b, p, q in zip(bs, zero_th, two):
            lifted[b, 0] = p
            lifted[b, 1] = q
        accumulate(0, bs, [dot(value, narrow_up[...]) for value in zero_th])
        accumulate(4, bs, [dot(value, narrow_up[...]) for value in two])

    def odd_tile(a, b):
        return dot(a, wide_up[:2 * LANES, :]) + dot(b, wide_up[2 * LANES:, :])

    def forward_second(b, split_at=None):
        recv_both(g_copy, 1, [b])
        one = lift(1, b)
        accumulate(1, [b], [odd_tile(lifted[b, 0], one)])
        accumulate(2, [b], [dot(one, narrow_up[...])])
        if split_at is not None:
            split_at()
        accumulate(3, [b], [odd_tile(one, lifted[b, 1])])

    def weighted(j, b):
        pieces = []
        for h, t in enumerate(lane_pair(j)):
            total = None
            for v in range(n_vars):
                p = pert[pl.ds(b * GROUP, GROUP), v, :, t * LANES:(t + 1) * LANES]
                term = p * misfit[h, flat_rows(j, v), :][None]
                total = term if total is None else total + term
            pieces.append(split(total.reshape(GROUP * fine, LANES)))
        lhs = jnp.concatenate([pieces[0][0], pieces[1][0], pieces[0][1], pieces[1][1]], axis=1)
        return dot(lhs, narrow_down[...] if j % 2 == 0 else wide_down[...])

    def lower(x):
        wide = dot(rows_down[...], both_pieces(x))
        return (wide[:, :LANES] + wide[:, LANES:]) * (1.0 / SCALE)

    def keep(b, rows, coarse):
        part_send[0, b, rows, :] = coarse[0]
        own[b, rows, :] = coarse[1]
        part_send[1, b, rows, :] = coarse[2]

    def three(x):
        return x[:seg], x[seg:2 * seg], x[2 * seg:]

    def adjoint_first(bs):
        for b in bs:
            last = weighted(4, b)
            wide = weighted(1, b)
            high = weighted(3, b)
            wrapped = jnp.where(lax.broadcasted_iota(jnp.int32, last.shape, 1) < LANES // 2, swap(last), 0.0)
            first = weighted(0, b) + wide[:, :LANES] + wrapped
            spare[b] = wide[:, LANES:] + high[:, :LANES]
            keep(b, first_rows, three(lower(first)))
            ends = three(lower(last + high[:, LANES:]))
            keep(b, tail_rows, [jnp.where(left, e[:half], swap(e[half:])) for e in ends])
        send_both(c_copy, 0, bs)

    def adjoint_second(bs):
        for b in bs:
            keep(b, second_rows, three(lower(spare[b] + weighted(2, b))))
        send_both(c_copy, 1, bs)

    def region(s):
        return pl.ds(bases[s], n_z * parts[s])

    def part_rows(s, at):
        return pl.ds(pl.multiple_of(bases[s] + at * parts[s], 8), parts[s])

    def pair_copy(s):
        return pltpu.make_async_remote_copy(
            src_ref=acc.at[1 - core, region(s)], dst_ref=pair_recv.at[region(s)],
            send_sem=p_ss.at[s], recv_sem=p_rs.at[s], device_id=partner, device_id_type=MESH)

    def z_copy(s, k):
        return pltpu.make_async_remote_copy(
            src_ref=half_sum.at[part_rows(s, lax.rem(z + k + 1, n_z))], dst_ref=z_recv.at[k, pl.ds(z_bases[s], parts[s])],
            send_sem=z_ss.at[s, k], recv_sem=z_rs.at[s, k], device_id=z_peers[k], device_id_type=MESH)

    def ag_copy(s, k, source):
        return pltpu.make_async_remote_copy(
            src_ref=image.at[core, part_rows(s, source)], dst_ref=image.at[core, part_rows(s, source)],
            send_sem=ag_ss.at[s, k], recv_sem=ag_rs.at[s, k], device_id=z_peers[k], device_id_type=MESH)

    def image_copy(index):
        return pltpu.make_async_remote_copy(
            src_ref=image.at[index], dst_ref=image.at[index],
            send_sem=im_ss.at[0], recv_sem=im_rs.at[0], device_id=partner, device_id_type=MESH)

    def pair_finish(s):
        pair_copy(s).wait_recv()
        half_sum[region(s), :] = acc[core, region(s), :] + pair_recv[region(s), :]
        for k in range(n_z - 1):
            z_copy(s, k).start()

    def z_finish(s):
        for k in range(n_z - 1):
            z_copy(s, k).wait_recv()
        total = half_sum[part_rows(s, z), :]
        for k in range(n_z - 1):
            total = total + z_recv[k, pl.ds(z_bases[s], parts[s]), :]
        total = total * (1.0 / SCALE)
        image[core, part_rows(s, z), :] = total
        if s < 2:
            gather_start(s)
        return total_of(total * total)

    def gather_start(s):
        for k in range(n_z - 1):
            ag_copy(s, k, z).start()

    def gather_pass():
        for s in range(3):
            for k in range(n_z - 1):
                ag_copy(s, k, lax.rem(z + n_z - 1 - k, n_z)).wait_recv()
        image_copy(core).start()

    def gather_finish():
        image_copy(1 - core).wait_recv()
        image_copy(core).wait_send()
        for s in range(3):
            pair_copy(s).wait_send()
            for k in range(n_z - 1):
                z_copy(s, k).wait_send()
                ag_copy(s, k, z).wait_send()

    def total_of(squares):
        return jnp.sum(squares.reshape(-1, 8, LANES), axis=0)

    def forward_all():
        acc[...] = jnp.zeros_like(acc)
        over_chunks(forward_first)
        pair_copy(0).start()

        def body(b, carry):
            forward_second(b)
            return carry

        lax.fori_loop(0, blocks - 1, body, 0)
        pair_finish(0)
        forward_second(blocks - 1, lambda: pair_copy(1).start())
        pair_copy(2).start()
        pair_finish(1)
        pair_finish(2)
        squares = z_finish(0)
        squares = squares + z_finish(1)
        squares = squares + z_finish(2)
        return squares

    def sl_copy(it, k):
        return pltpu.make_async_remote_copy(
            src_ref=lat_send, dst_ref=lat_recv.at[it, k],
            send_sem=sl_ss.at[it, k], recv_sem=sl_rs.at[it, k], device_id=lat_peers[k], device_id_type=MESH)

    def sm_copy(it, k):
        return pltpu.make_async_remote_copy(
            src_ref=mem_send, dst_ref=mem_recv.at[it, k],
            send_sem=sm_ss.at[it, k], recv_sem=sm_rs.at[it, k], device_id=mem_peers[k], device_id_type=MESH)

    loads[0].wait()
    for b in range(blocks):
        block = control[:, pl.ds(b * GROUP, GROUP), :].reshape(seg, control.shape[2])
        ends = block[:, 2 * LANES:]
        tail = jnp.concatenate([ends[:half], ends[half:]], axis=1)
        for rows, value in ((first_rows, block[:, :LANES]), (second_rows, block[:, LANES:2 * LANES]), (tail_rows, tail)):
            halo[1, b, rows, :] = value
            w[b, rows, :] = value

    pl.semaphore_wait(barrier, len(lat_peers) + len(mem_peers))
    over_chunks(functools.partial(send_both, g_copy, 0))
    over_chunks(functools.partial(send_both, g_copy, 1))

    zero = jnp.zeros(halo.shape[2:], jnp.float32)

    @pl.when(jnp.logical_not(has_up))
    def _():
        for b in range(blocks):
            halo[0, b] = zero
            part_recv[1, b] = zero

    @pl.when(jnp.logical_not(has_down))
    def _():
        for b in range(blocks):
            halo[2, b] = zero
            part_recv[0, b] = zero

    for load in loads[1:]:
        load.wait()
    for j in range(pairs):
        for h, t in enumerate(lane_pair(j)):
            for v in range(n_vars):
                obs[h, flat_rows(j, v), :] = innov[v, :, t * LANES:(t + 1) * LANES]
    for c in range(blocks):
        pert_copy(c).wait()

    def widen(m, carry):
        pert[m] = pert_raw[m].astype(jnp.float32)
        return carry

    lax.fori_loop(0, pert.shape[0], widen, 0)
    forward_all()
    gather_start(2)
    sent_all(g_copy)
    gather_pass()
    gather_finish()
    inc[...] = image[...]

    def step(it, step_len):
        for h in range(2):
            for j in (4, 0, 1, 3, 2):
                for v in range(n_vars):
                    rows = flat_rows(j, v)
                    moved = inc[h, rows, :] - step_len * image[h, rows, :]
                    inc[h, rows, :] = moved
                    misfit[h, rows, :] = jnp.clip(moved - obs[h, rows, :], -thr[v], thr[v])
        for bs in ((0,), (1,), (2,), (3,)):
            adjoint_first(bs)
        over_chunks(adjoint_second)
        for b in range(blocks):
            w[b] = w[b] - step_len * halo[1, b]

        def gradient(q):
            def body(b, squares):
                recv_both(c_copy, q, [b])
                rows = pl.ds(*groups[q])
                grad = w[b, rows, :] + own[b, rows, :] + part_recv[0, b, rows, :] + part_recv[1, b, rows, :]
                halo[1, b, rows, :] = grad
                send_both(g_copy, q, [b])
                return squares + total_of(grad * grad)

            return lax.fori_loop(0, blocks, body, jnp.zeros((8, LANES), jnp.float32))

        grad_sq = gradient(0)
        grad_sq = grad_sq + gradient(1)
        image_sq = forward_all()
        sums = jnp.concatenate([jnp.sum(grad_sq, axis=0, keepdims=True), jnp.sum(image_sq, axis=0, keepdims=True)], axis=0)
        mem_send[...] = sums
        for k in range(n_mem - 1):
            sm_copy(it, k).start()
        gather_start(2)
        sent_all(c_copy)
        sent_all(g_copy)
        for k in range(n_mem - 1):
            sm_copy(it, k).wait_recv()
        sums = sums + jnp.sum(mem_recv[it], axis=0)
        lat_send[...] = sums
        for k in range(n_lat - 1):
            sl_copy(it, k).start()
        gather_pass()
        gather_finish()
        for k in range(n_lat - 1):
            sl_copy(it, k).wait_recv()
        sums = sums + jnp.sum(lat_recv[it], axis=0)
        for k in range(n_lat - 1):
            sl_copy(it, k).wait_send()
        g2 = jnp.sum(sums[0:1, :], axis=1, keepdims=True)
        h2 = jnp.sum(sums[1:2, :], axis=1, keepdims=True)
        step_len = g2 / (g2 + h2)
        for k in range(n_mem - 1):
            sm_copy(it, k).wait_send()
        return step_len

    step_len = lax.fori_loop(0, STEPS, step, jnp.zeros((1, 1), jnp.float32))

    for b in range(blocks):
        members = pl.ds(b * GROUP, GROUP)
        final = w[b] - step_len * halo[1, b]
        one, tail, two = final[:seg], final[seg:seg + half], final[seg + half:]
        weights_out[:, members, :LANES] = one.reshape(n_rows, GROUP, LANES)
        weights_out[:, members, LANES:2 * LANES] = two.reshape(n_rows, GROUP, LANES)
        weights_out[:n_rows // 2, members, 2 * LANES:] = tail[:, :LANES // 2].reshape(n_rows // 2, GROUP, LANES // 2)
        weights_out[n_rows // 2:, members, 2 * LANES:] = tail[:, LANES // 2:].reshape(n_rows // 2, GROUP, LANES // 2)

    share = inc_out.shape[2]
    first = mem * share // LANES
    shift = mem * share - first * LANES

    def lane_tile(t, v):
        j = jnp.where(t % 2 == 1, (t - 1) // 2, (t // 2 + pairs - 1) % pairs)
        row = jnp.int32(0)
        for i in range(pairs):
            row = jnp.where(j == i, starts[i] + v * fine, row)
        rows = pl.ds(pl.multiple_of(row, 8), fine)
        return inc[1 - t % 2, rows, :] - step_len * image[1 - t % 2, rows, :]

    fine_lane = lax.broadcasted_iota(jnp.int32, (fine, LANES), 1)
    for v in range(n_vars):
        a = pltpu.roll(lane_tile(first, v), (LANES - shift) % LANES, 1)
        b = pltpu.roll(lane_tile(first + 1, v), (LANES - shift) % LANES, 1)
        inc_out[v, :, :LANES] = jnp.where(fine_lane < LANES - shift, a, b)
        inc_out[v, :, LANES:] = b[:, :share - LANES]


def copy_kernel(a_ref, b_ref, c_ref, d_ref, sems):
    copies = [pltpu.make_async_copy(a_ref, c_ref, sems.at[0]), pltpu.make_async_copy(b_ref, d_ref, sems.at[1])]
    for copy in copies:
        copy.start()
    for copy in copies:
        copy.wait()


def per_device(n_mem, n_lat, perturbations, control, innovations, thresholds):
    members, coarse_rows, coarse_cols = control.shape
    n_vars, fine_rows, fine_cols = innovations.shape
    blocks = members // GROUP
    seg = GROUP * coarse_rows
    packed = seg * coarse_cols // LANES
    n_z = n_mem // 2
    tile_rows = n_vars * fine_rows
    pairs = fine_cols // (2 * LANES)
    parts, bases, flat = [], [], 0
    starts = [0] * pairs
    for tiles in ((0, 4), (1, 2), (3,)):
        parts.append(-(-len(tiles) * tile_rows // n_z // 8) * 8)
        bases.append(flat)
        for i, j in enumerate(tiles):
            starts[j] = flat + i * tile_rows
        flat += n_z * parts[-1]
    vmem = pl.BlockSpec(memory_space=pltpu.VMEM)
    whole = pl.BlockSpec(memory_space=pl.ANY)
    f32 = jnp.float32
    bf16 = jnp.bfloat16
    dma = pltpu.SemaphoreType.DMA
    constants = tables(coarse_rows)
    ordered = control.transpose(1, 0, 2)
    shapes = (
        jax.ShapeDtypeStruct(ordered.shape, f32),
        jax.ShapeDtypeStruct((n_vars, fine_rows, fine_cols // n_mem), f32))
    weights, increment = pl.pallas_call(
        functools.partial(kernel, n_mem, n_lat, seg, (bases, parts, starts)),
        out_shape=tuple(pltpu.VMEM(x.shape, f32) for x in shapes),
        in_specs=[whole] * 10,
        out_specs=(vmem, vmem),
        scratch_shapes=[
            pltpu.SMEM(thresholds.shape, f32),
            pltpu.VMEM(perturbations.shape, bf16),
            pltpu.VMEM(perturbations.shape, f32),
            pltpu.VMEM(ordered.shape, f32),
            pltpu.VMEM(innovations.shape, f32),
            pltpu.VMEM(constants[0].shape[1:], bf16),
            pltpu.VMEM(constants[1].shape[1:], bf16),
            pltpu.VMEM(constants[2].shape, bf16),
            pltpu.VMEM(constants[3].shape, bf16),
            pltpu.VMEM(constants[4].shape, bf16),
            pltpu.VMEM(constants[5].shape, bf16),
            pltpu.VMEM((3, blocks, packed, LANES), f32),
            pltpu.VMEM((2, blocks, packed, LANES), f32),
            pltpu.VMEM((2, blocks, packed, LANES), f32),
            pltpu.VMEM((blocks, packed, LANES), f32),
            pltpu.VMEM((blocks, packed, LANES), f32),
            pltpu.VMEM((blocks, GROUP * fine_rows, LANES), f32),
            pltpu.VMEM((blocks, 2, GROUP * fine_rows, 2 * LANES), bf16),
            pltpu.VMEM((2, flat, LANES), f32),
            pltpu.VMEM((flat, LANES), f32),
            pltpu.VMEM((flat, LANES), f32),
            pltpu.VMEM((n_z - 1, sum(parts), LANES), f32),
            pltpu.VMEM((2, flat, LANES), f32),
            pltpu.VMEM((2, flat, LANES), f32),
            pltpu.VMEM((2, flat, LANES), f32),
            pltpu.VMEM((2, flat, LANES), f32),
            pltpu.VMEM((2, LANES), f32),
            pltpu.VMEM((STEPS, n_lat - 1, 2, LANES), f32),
            pltpu.VMEM((2, LANES), f32),
            pltpu.VMEM((STEPS, n_mem - 1, 2, LANES), f32),
            dma((blocks,)), dma((9,)),
            dma((2, 2, blocks)), dma((2, 2, blocks)), dma((2, 2, blocks)), dma((2, 2, blocks)),
            dma((3,)), dma((3,)), dma((3, n_z - 1)), dma((3, n_z - 1)), dma((3, n_z - 1)), dma((3, n_z - 1)), dma((1,)), dma((1,)),
            dma((STEPS, n_lat - 1)), dma((STEPS, n_lat - 1)), dma((STEPS, n_mem - 1)), dma((STEPS, n_mem - 1)),
        ],
        compiler_params=pltpu.CompilerParams(collective_id=0, has_side_effects=True),
    )(perturbations, ordered, innovations, thresholds, *constants)
    weights, increment = pl.pallas_call(
        copy_kernel, out_shape=shapes, in_specs=[vmem] * 2, out_specs=(whole, whole),
        scratch_shapes=[dma((2,))])(pltpu.with_memory_space_constraint(weights, pltpu.VMEM), pltpu.with_memory_space_constraint(increment, pltpu.VMEM))
    return weights.transpose(1, 0, 2), increment


def solution(mesh):
    return jax.shard_map(
        functools.partial(per_device, mesh.shape["mem"], mesh.shape["lat"]),
        mesh=mesh,
        in_specs=(P("mem", None, "lat", None), P("mem", "lat", None), P(None, "lat", None), P()),
        out_specs=(P("mem", "lat", None), P(None, "lat", "mem")),
        check_vma=False,
    )
```

```python
import functools

import jax
import jax.numpy as jnp
import numpy as np
from jax import lax
from jax.experimental import pallas as pl
from jax.experimental.pallas import tpu as pltpu
from jax.sharding import PartitionSpec as P

RATIO = 4
HALF = 5
STEPS = 2
SIDE = 4
GROUP = 8
PAIR = 2
LANES = 128
MESH = pl.DeviceIdType.MESH
SCALE = 96.0


def tent(distance):
    return np.maximum(0.0, 1.0 - np.abs(distance) / RATIO)


def row_operator(coarse_rows, first, last):
    fine = np.arange(RATIO * coarse_rows)[:, None]
    inner = np.arange(-1, coarse_rows + 1)
    up = tent(fine + 0.5 - RATIO * inner[None, :] - RATIO / 2)
    if first:
        up[:, 0] = 0.0
    if last:
        up[:, -1] = 0.0
    outer = np.arange(-coarse_rows, 2 * coarse_rows)
    gap = np.abs(inner[:, None] - outer[None, :])
    smooth = np.where(gap <= HALF, (1.0 - gap / (HALF + 1)) / 2, 0.0)
    return np.rint(SCALE * up @ smooth)


def block_rows(operator):
    fine, wide = operator.shape
    out = np.zeros((GROUP, fine, wide, GROUP))
    for member in range(GROUP):
        out[member, :, :, member] = operator
    return out.reshape(GROUP * fine, wide * GROUP)


def tables(coarse_rows):
    ops = [block_rows(row_operator(coarse_rows, *ends)) for ends in ((True, False), (False, False), (False, True))]
    rows_up = np.stack(ops)
    rows_down = np.stack([op.T for op in ops])
    fine = np.arange(2 * LANES)[None, :]
    narrow = tent(LANES + fine + 0.5 - RATIO * np.arange(LANES)[:, None] - RATIO / 2)
    wide = tent(3 * LANES + fine + 0.5 - RATIO * np.arange(2 * LANES)[:, None] - RATIO / 2)
    narrow_up = np.concatenate([narrow, narrow], 0)
    wide_up = np.concatenate([wide[:LANES], wide[:LANES], wide[LANES:], wide[LANES:]], 0)
    narrow_down = np.concatenate([narrow.T, narrow.T], 0)
    wide_down = np.concatenate([wide.T, wide.T], 0)
    return [jnp.asarray(t, jnp.bfloat16) for t in (rows_up, rows_down, narrow_up, wide_up, narrow_down, wide_down)]


def split(x):
    high = x.astype(jnp.bfloat16)
    return high, (x - high.astype(jnp.float32)).astype(jnp.bfloat16)


def dot(a, b):
    return jnp.dot(a, b, preferred_element_type=jnp.float32)


def kernel(
    n_mem, n_lat, seg, layout,
    pert_hbm, control_hbm, innov_hbm, thr_hbm, rows_up_hbm, rows_down_hbm, narrow_up_hbm, wide_up_hbm, narrow_down_hbm, wide_down_hbm,
    weights_out, inc_out,
    thr, pert_raw, pert, control, innov, rows_up, rows_down, narrow_up, wide_up, narrow_down, wide_down,
    halo, part_send, part_recv, own, w, spare, lifted, acc, pair_recv, half_sum, z_recv, image, inc, misfit, obs,
    lat_send, lat_recv, mem_send, mem_recv,
    pert_sem, load_sem, g_send, g_recv, c_send, c_recv, p_ss, p_rs, z_ss, z_rs, ag_ss, ag_rs, im_ss, im_rs, sl_ss, sl_rs, sm_ss, sm_rs,
):
    mem = lax.axis_index("mem")
    lat = lax.axis_index("lat")
    core = lax.rem(mem, 2)
    n_z = n_mem // 2
    z = mem // 2
    blocks = pert.shape[0] // GROUP
    chunks = blocks // PAIR
    n_vars = pert.shape[1]
    fine = pert.shape[2]
    tiles = pert.shape[3] // LANES
    pairs = tiles // 2
    tile_rows = n_vars * fine
    half = seg // 2
    n_rows = seg // GROUP
    case = jnp.where(lat == 0, 0, jnp.where(lat == n_lat - 1, 2, 1))
    up_id = (mem, jnp.maximum(lat - 1, 0))
    down_id = (mem, jnp.minimum(lat + 1, n_lat - 1))
    has_up = lat > 0
    has_down = lat < n_lat - 1
    partner = (2 * z + 1 - core, lat)
    z_peers = [(2 * lax.rem(z + k, n_z) + core, lat) for k in range(1, n_z)]
    mem_peers = [(2 * lax.rem(z + k, n_z) + c, lat) for k in (2, 1, 3) for c in (core, 1 - core)] + [partner]
    far = sorted(((i, k) for i in range(SIDE) for k in range(SIDE) if i or k), key=lambda at: -sum(min(d, SIDE - d) for d in at))
    lat_peers = [(mem, lax.rem(lat // SIDE + i, SIDE) * SIDE + lax.rem(lat + k, SIDE)) for i, k in far]
    groups = ((0, seg + half), (seg + half, seg))
    first_rows, tail_rows, second_rows = pl.ds(0, seg), pl.ds(seg, half), pl.ds(seg + half, seg)
    bases, parts, starts = layout
    z_order = sorted(range(n_z - 1), key=lambda k: k + 1 != n_z // 2)
    z_bases = [sum(parts[:i]) for i in range(3)]

    loads = [
        (control_hbm, control), (rows_up_hbm.at[case], rows_up), (narrow_up_hbm, narrow_up), (wide_up_hbm, wide_up),
        (innov_hbm, innov), (rows_down_hbm.at[case], rows_down), (narrow_down_hbm, narrow_down), (wide_down_hbm, wide_down),
        (thr_hbm, thr),
    ]
    loads = [pltpu.make_async_copy(src, dst, load_sem.at[i]) for i, (src, dst) in enumerate(loads)]

    loads[0].start()
    barrier = pltpu.get_barrier_semaphore()
    for peer in lat_peers + mem_peers:
        pl.semaphore_signal(barrier, inc=1, device_id=peer, device_id_type=MESH)

    def pert_copy(c):
        rows = pl.ds(c * GROUP, GROUP)
        return pltpu.make_async_copy(pert_hbm.at[rows], pert_raw.at[rows], pert_sem.at[c])

    for load in loads[1:4]:
        load.start()
    for c in range(blocks):
        pert_copy(c).start()
    for load in loads[4:]:
        load.start()

    lane = lax.broadcasted_iota(jnp.int32, (half, LANES), 1)
    left = lane < LANES // 2

    def swap(x):
        return pltpu.roll(x, LANES // 2, 1)

    def g_copy(q, b, up):
        rows = pl.ds(*groups[q])
        i = 0 if up else 1
        return pltpu.make_async_remote_copy(
            src_ref=halo.at[1, b, rows], dst_ref=halo.at[2 if up else 0, b, rows],
            send_sem=g_send.at[i, q, b], recv_sem=g_recv.at[i, q, b],
            device_id=up_id if up else down_id, device_id_type=MESH)

    def c_copy(q, b, up):
        rows = pl.ds(*groups[q])
        i = 0 if up else 1
        return pltpu.make_async_remote_copy(
            src_ref=part_send.at[i, b, rows], dst_ref=part_recv.at[i, b, rows],
            send_sem=c_send.at[i, q, b], recv_sem=c_recv.at[i, q, b],
            device_id=up_id if up else down_id, device_id_type=MESH)

    def send_both(copy, q, bs):
        @pl.when(has_up)
        def _():
            for b in bs:
                copy(q, b, True).start()

        @pl.when(has_down)
        def _():
            for b in bs:
                copy(q, b, False).start()

    def recv_both(copy, q, bs):
        @pl.when(has_down)
        def _():
            for b in bs:
                copy(q, b, True).wait_recv()

        @pl.when(has_up)
        def _():
            for b in bs:
                copy(q, b, False).wait_recv()

    def sent_all(copy):
        def body(b, carry):
            for q in range(2):
                @pl.when(has_up)
                def _():
                    copy(q, b, True).wait_send()

                @pl.when(has_down)
                def _():
                    copy(q, b, False).wait_send()
            return carry

        lax.fori_loop(0, blocks, body, 0)

    def over_chunks(f):
        def body(c, carry):
            f([c * PAIR + i for i in range(PAIR)])
            return carry

        lax.fori_loop(0, chunks, body, 0)

    def lane_pair(j):
        return 2 * j + 1, (2 * j + 2) % tiles

    def flat_rows(j, v):
        return pl.ds(starts[j] + v * fine, fine)

    def both_pieces(x):
        high, low = split(x)
        return jnp.concatenate([high, low], axis=1)

    def lift(g, b):
        pieces = []
        for i in range(3):
            if g < 2:
                pieces.append(halo[i, b, second_rows if g else first_rows, :])
            else:
                first = halo[i, b, first_rows, :]
                tail = halo[i, b, tail_rows, :]
                pieces.append(jnp.where(left, tail, swap(first[:half])))
                pieces.append(jnp.where(left, swap(tail), swap(first[half:])))
        wide = dot(rows_up[...], both_pieces(jnp.concatenate(pieces, axis=0)))
        return both_pieces(wide[:, :LANES] + wide[:, LANES:])

    def accumulate(j, bs, fields):
        for h, t in enumerate(lane_pair(j)):
            for v in range(n_vars):
                total = acc[h, flat_rows(j, v), :]
                for b, field in zip(bs, fields):
                    f = field[:, h * LANES:(h + 1) * LANES].reshape(GROUP, fine, LANES)
                    p = pert[pl.ds(b * GROUP, GROUP), v, :, t * LANES:(t + 1) * LANES]
                    total = total + jnp.sum(p * f, axis=0)
                acc[h, flat_rows(j, v), :] = total

    def forward_first(bs):
        recv_both(g_copy, 0, bs)
        zero_th = [lift(0, b) for b in bs]
        two = [lift(2, b) for b in bs]
        for b, p, q in zip(bs, zero_th, two):
            lifted[b, 0] = p
            lifted[b, 1] = q
        accumulate(0, bs, [dot(value, narrow_up[...]) for value in zero_th])
        accumulate(4, bs, [dot(value, narrow_up[...]) for value in two])

    def odd_tile(a, b):
        return dot(a, wide_up[:2 * LANES, :]) + dot(b, wide_up[2 * LANES:, :])

    def forward_second(b, split_at=None):
        recv_both(g_copy, 1, [b])
        one = lift(1, b)
        accumulate(1, [b], [odd_tile(lifted[b, 0], one)])
        accumulate(2, [b], [dot(one, narrow_up[...])])
        if split_at is not None:
            split_at()
        accumulate(3, [b], [odd_tile(one, lifted[b, 1])])

    def weighted(j, b):
        pieces = []
        for h, t in enumerate(lane_pair(j)):
            total = None
            for v in range(n_vars):
                p = pert[pl.ds(b * GROUP, GROUP), v, :, t * LANES:(t + 1) * LANES]
                term = p * misfit[h, flat_rows(j, v), :][None]
                total = term if total is None else total + term
            pieces.append(split(total.reshape(GROUP * fine, LANES)))
        lhs = jnp.concatenate([pieces[0][0], pieces[1][0], pieces[0][1], pieces[1][1]], axis=1)
        return dot(lhs, narrow_down[...] if j % 2 == 0 else wide_down[...])

    def lower(x):
        wide = dot(rows_down[...], both_pieces(x))
        return (wide[:, :LANES] + wide[:, LANES:]) * (1.0 / SCALE)

    def keep(b, rows, coarse):
        part_send[0, b, rows, :] = coarse[0]
        own[b, rows, :] = coarse[1]
        part_send[1, b, rows, :] = coarse[2]

    def three(x):
        return x[:seg], x[seg:2 * seg], x[2 * seg:]

    def adjoint_first(bs):
        for b in bs:
            last = weighted(4, b)
            wide = weighted(1, b)
            high = weighted(3, b)
            wrapped = jnp.where(lax.broadcasted_iota(jnp.int32, last.shape, 1) < LANES // 2, swap(last), 0.0)
            first = weighted(0, b) + wide[:, :LANES] + wrapped
            spare[b] = wide[:, LANES:] + high[:, :LANES]
            keep(b, first_rows, three(lower(first)))
            ends = three(lower(last + high[:, LANES:]))
            keep(b, tail_rows, [jnp.where(left, e[:half], swap(e[half:])) for e in ends])
        send_both(c_copy, 0, bs)

    def adjoint_second(bs):
        for b in bs:
            keep(b, second_rows, three(lower(spare[b] + weighted(2, b))))
        send_both(c_copy, 1, bs)

    def region(s):
        return pl.ds(bases[s], n_z * parts[s])

    def part_rows(s, at):
        return pl.ds(pl.multiple_of(bases[s] + at * parts[s], 8), parts[s])

    def pair_copy(s):
        return pltpu.make_async_remote_copy(
            src_ref=acc.at[1 - core, region(s)], dst_ref=pair_recv.at[region(s)],
            send_sem=p_ss.at[s], recv_sem=p_rs.at[s], device_id=partner, device_id_type=MESH)

    def z_copy(s, k):
        return pltpu.make_async_remote_copy(
            src_ref=half_sum.at[part_rows(s, lax.rem(z + k + 1, n_z))], dst_ref=z_recv.at[k, pl.ds(z_bases[s], parts[s])],
            send_sem=z_ss.at[s, k], recv_sem=z_rs.at[s, k], device_id=z_peers[k], device_id_type=MESH)

    def ag_copy(s, k, source):
        return pltpu.make_async_remote_copy(
            src_ref=image.at[core, part_rows(s, source)], dst_ref=image.at[core, part_rows(s, source)],
            send_sem=ag_ss.at[s, k], recv_sem=ag_rs.at[s, k], device_id=z_peers[k], device_id_type=MESH)

    def image_copy(index):
        return pltpu.make_async_remote_copy(
            src_ref=image.at[index], dst_ref=image.at[index],
            send_sem=im_ss.at[0], recv_sem=im_rs.at[0], device_id=partner, device_id_type=MESH)

    def pair_finish(s):
        pair_copy(s).wait_recv()
        half_sum[region(s), :] = acc[core, region(s), :] + pair_recv[region(s), :]
        for k in z_order:
            z_copy(s, k).start()

    def z_finish(s):
        for k in range(n_z - 1):
            z_copy(s, k).wait_recv()
        total = half_sum[part_rows(s, z), :]
        for k in range(n_z - 1):
            total = total + z_recv[k, pl.ds(z_bases[s], parts[s]), :]
        total = total * (1.0 / SCALE)
        image[core, part_rows(s, z), :] = total
        if s < 2:
            gather_start(s)
        return total_of(total * total)

    def gather_start(s):
        for k in z_order:
            ag_copy(s, k, z).start()

    def gather_pass():
        for s in range(3):
            for k in range(n_z - 1):
                ag_copy(s, k, lax.rem(z + n_z - 1 - k, n_z)).wait_recv()
        image_copy(core).start()

    def gather_finish():
        image_copy(1 - core).wait_recv()
        image_copy(core).wait_send()
        for s in range(3):
            pair_copy(s).wait_send()
            for k in range(n_z - 1):
                z_copy(s, k).wait_send()
                ag_copy(s, k, z).wait_send()

    def total_of(squares):
        return jnp.sum(squares.reshape(-1, 8, LANES), axis=0)

    def forward_all():
        acc[...] = jnp.zeros_like(acc)
        over_chunks(forward_first)
        pair_copy(0).start()

        def body(b, carry):
            forward_second(b)
            return carry

        lax.fori_loop(0, blocks - 1, body, 0)
        pair_finish(0)
        forward_second(blocks - 1, lambda: pair_copy(1).start())
        pair_copy(2).start()
        pair_finish(1)
        pair_finish(2)
        squares = z_finish(0)
        squares = squares + z_finish(1)
        squares = squares + z_finish(2)
        return squares

    def sl_copy(it, k):
        return pltpu.make_async_remote_copy(
            src_ref=lat_send, dst_ref=lat_recv.at[it, k],
            send_sem=sl_ss.at[it, k], recv_sem=sl_rs.at[it, k], device_id=lat_peers[k], device_id_type=MESH)

    def sm_copy(it, k):
        return pltpu.make_async_remote_copy(
            src_ref=mem_send, dst_ref=mem_recv.at[it, k],
            send_sem=sm_ss.at[it, k], recv_sem=sm_rs.at[it, k], device_id=mem_peers[k], device_id_type=MESH)

    loads[0].wait()
    for b in range(blocks):
        block = control[:, pl.ds(b * GROUP, GROUP), :].reshape(seg, control.shape[2])
        ends = block[:, 2 * LANES:]
        tail = jnp.concatenate([ends[:half], ends[half:]], axis=1)
        for rows, value in ((first_rows, block[:, :LANES]), (second_rows, block[:, LANES:2 * LANES]), (tail_rows, tail)):
            halo[1, b, rows, :] = value
            w[b, rows, :] = value

    pl.semaphore_wait(barrier, len(lat_peers) + len(mem_peers))
    over_chunks(functools.partial(send_both, g_copy, 0))
    over_chunks(functools.partial(send_both, g_copy, 1))

    zero = jnp.zeros(halo.shape[2:], jnp.float32)

    @pl.when(jnp.logical_not(has_up))
    def _():
        for b in range(blocks):
            halo[0, b] = zero
            part_recv[1, b] = zero

    @pl.when(jnp.logical_not(has_down))
    def _():
        for b in range(blocks):
            halo[2, b] = zero
            part_recv[0, b] = zero

    for load in loads[1:]:
        load.wait()
    for j in range(pairs):
        for h, t in enumerate(lane_pair(j)):
            for v in range(n_vars):
                obs[h, flat_rows(j, v), :] = innov[v, :, t * LANES:(t + 1) * LANES]
    for c in range(blocks):
        pert_copy(c).wait()

    def widen(m, carry):
        pert[m] = pert_raw[m].astype(jnp.float32)
        return carry

    lax.fori_loop(0, pert.shape[0], widen, 0)
    forward_all()
    gather_start(2)
    sent_all(g_copy)
    gather_pass()
    gather_finish()
    inc[...] = image[...]

    def step(it, step_len):
        for h in range(2):
            for j in (4, 0, 1, 3, 2):
                for v in range(n_vars):
                    rows = flat_rows(j, v)
                    moved = inc[h, rows, :] - step_len * image[h, rows, :]
                    inc[h, rows, :] = moved
                    misfit[h, rows, :] = jnp.clip(moved - obs[h, rows, :], -thr[v], thr[v])
        for bs in ((0,), (1,), (2,), (3,)):
            adjoint_first(bs)
        over_chunks(adjoint_second)
        for b in range(blocks):
            w[b] = w[b] - step_len * halo[1, b]

        def gradient(q):
            def body(b, squares):
                recv_both(c_copy, q, [b])
                rows = pl.ds(*groups[q])
                grad = w[b, rows, :] + own[b, rows, :] + part_recv[0, b, rows, :] + part_recv[1, b, rows, :]
                halo[1, b, rows, :] = grad
                send_both(g_copy, q, [b])
                return squares + total_of(grad * grad)

            return lax.fori_loop(0, blocks, body, jnp.zeros((8, LANES), jnp.float32))

        grad_sq = gradient(0)
        grad_sq = grad_sq + gradient(1)
        image_sq = forward_all()
        sums = jnp.concatenate([jnp.sum(grad_sq, axis=0, keepdims=True), jnp.sum(image_sq, axis=0, keepdims=True)], axis=0)
        mem_send[...] = sums
        for k in range(n_mem - 1):
            sm_copy(it, k).start()
        gather_start(2)
        sent_all(c_copy)
        sent_all(g_copy)
        for k in range(n_mem - 1):
            sm_copy(it, k).wait_recv()
        sums = sums + jnp.sum(mem_recv[it], axis=0)
        lat_send[...] = sums
        for k in range(n_lat - 1):
            sl_copy(it, k).start()
        gather_pass()
        gather_finish()
        for k in range(n_lat - 1):
            sl_copy(it, k).wait_recv()
        sums = sums + jnp.sum(lat_recv[it], axis=0)
        for k in range(n_lat - 1):
            sl_copy(it, k).wait_send()
        g2 = jnp.sum(sums[0:1, :], axis=1, keepdims=True)
        h2 = jnp.sum(sums[1:2, :], axis=1, keepdims=True)
        step_len = g2 / (g2 + h2)
        for k in range(n_mem - 1):
            sm_copy(it, k).wait_send()
        return step_len

    step_len = lax.fori_loop(0, STEPS, step, jnp.zeros((1, 1), jnp.float32))

    for b in range(blocks):
        members = pl.ds(b * GROUP, GROUP)
        final = w[b] - step_len * halo[1, b]
        one, tail, two = final[:seg], final[seg:seg + half], final[seg + half:]
        weights_out[:, members, :LANES] = one.reshape(n_rows, GROUP, LANES)
        weights_out[:, members, LANES:2 * LANES] = two.reshape(n_rows, GROUP, LANES)
        weights_out[:n_rows // 2, members, 2 * LANES:] = tail[:, :LANES // 2].reshape(n_rows // 2, GROUP, LANES // 2)
        weights_out[n_rows // 2:, members, 2 * LANES:] = tail[:, LANES // 2:].reshape(n_rows // 2, GROUP, LANES // 2)

    share = inc_out.shape[2]
    first = mem * share // LANES
    shift = mem * share - first * LANES

    def lane_tile(t, v):
        j = jnp.where(t % 2 == 1, (t - 1) // 2, (t // 2 + pairs - 1) % pairs)
        row = jnp.int32(0)
        for i in range(pairs):
            row = jnp.where(j == i, starts[i] + v * fine, row)
        rows = pl.ds(pl.multiple_of(row, 8), fine)
        return inc[1 - t % 2, rows, :] - step_len * image[1 - t % 2, rows, :]

    fine_lane = lax.broadcasted_iota(jnp.int32, (fine, LANES), 1)
    for v in range(n_vars):
        a = pltpu.roll(lane_tile(first, v), (LANES - shift) % LANES, 1)
        b = pltpu.roll(lane_tile(first + 1, v), (LANES - shift) % LANES, 1)
        inc_out[v, :, :LANES] = jnp.where(fine_lane < LANES - shift, a, b)
        inc_out[v, :, LANES:] = b[:, :share - LANES]


def copy_kernel(a_ref, b_ref, c_ref, d_ref, sems):
    copies = [pltpu.make_async_copy(a_ref, c_ref, sems.at[0]), pltpu.make_async_copy(b_ref, d_ref, sems.at[1])]
    for copy in copies:
        copy.start()
    for copy in copies:
        copy.wait()


def per_device(n_mem, n_lat, perturbations, control, innovations, thresholds):
    members, coarse_rows, coarse_cols = control.shape
    n_vars, fine_rows, fine_cols = innovations.shape
    blocks = members // GROUP
    seg = GROUP * coarse_rows
    packed = seg * coarse_cols // LANES
    n_z = n_mem // 2
    tile_rows = n_vars * fine_rows
    pairs = fine_cols // (2 * LANES)
    parts, bases, flat = [], [], 0
    starts = [0] * pairs
    for tiles in ((0, 4), (1, 2), (3,)):
        parts.append(-(-len(tiles) * tile_rows // n_z // 8) * 8)
        bases.append(flat)
        for i, j in enumerate(tiles):
            starts[j] = flat + i * tile_rows
        flat += n_z * parts[-1]
    vmem = pl.BlockSpec(memory_space=pltpu.VMEM)
    whole = pl.BlockSpec(memory_space=pl.ANY)
    f32 = jnp.float32
    bf16 = jnp.bfloat16
    dma = pltpu.SemaphoreType.DMA
    constants = tables(coarse_rows)
    ordered = control.transpose(1, 0, 2)
    shapes = (
        jax.ShapeDtypeStruct(ordered.shape, f32),
        jax.ShapeDtypeStruct((n_vars, fine_rows, fine_cols // n_mem), f32))
    weights, increment = pl.pallas_call(
        functools.partial(kernel, n_mem, n_lat, seg, (bases, parts, starts)),
        out_shape=tuple(pltpu.VMEM(x.shape, f32) for x in shapes),
        in_specs=[whole] * 10,
        out_specs=(vmem, vmem),
        scratch_shapes=[
            pltpu.SMEM(thresholds.shape, f32),
            pltpu.VMEM(perturbations.shape, bf16),
            pltpu.VMEM(perturbations.shape, f32),
            pltpu.VMEM(ordered.shape, f32),
            pltpu.VMEM(innovations.shape, f32),
            pltpu.VMEM(constants[0].shape[1:], bf16),
            pltpu.VMEM(constants[1].shape[1:], bf16),
            pltpu.VMEM(constants[2].shape, bf16),
            pltpu.VMEM(constants[3].shape, bf16),
            pltpu.VMEM(constants[4].shape, bf16),
            pltpu.VMEM(constants[5].shape, bf16),
            pltpu.VMEM((3, blocks, packed, LANES), f32),
            pltpu.VMEM((2, blocks, packed, LANES), f32),
            pltpu.VMEM((2, blocks, packed, LANES), f32),
            pltpu.VMEM((blocks, packed, LANES), f32),
            pltpu.VMEM((blocks, packed, LANES), f32),
            pltpu.VMEM((blocks, GROUP * fine_rows, LANES), f32),
            pltpu.VMEM((blocks, 2, GROUP * fine_rows, 2 * LANES), bf16),
            pltpu.VMEM((2, flat, LANES), f32),
            pltpu.VMEM((flat, LANES), f32),
            pltpu.VMEM((flat, LANES), f32),
            pltpu.VMEM((n_z - 1, sum(parts), LANES), f32),
            pltpu.VMEM((2, flat, LANES), f32),
            pltpu.VMEM((2, flat, LANES), f32),
            pltpu.VMEM((2, flat, LANES), f32),
            pltpu.VMEM((2, flat, LANES), f32),
            pltpu.VMEM((2, LANES), f32),
            pltpu.VMEM((STEPS, n_lat - 1, 2, LANES), f32),
            pltpu.VMEM((2, LANES), f32),
            pltpu.VMEM((STEPS, n_mem - 1, 2, LANES), f32),
            dma((blocks,)), dma((9,)),
            dma((2, 2, blocks)), dma((2, 2, blocks)), dma((2, 2, blocks)), dma((2, 2, blocks)),
            dma((3,)), dma((3,)), dma((3, n_z - 1)), dma((3, n_z - 1)), dma((3, n_z - 1)), dma((3, n_z - 1)), dma((1,)), dma((1,)),
            dma((STEPS, n_lat - 1)), dma((STEPS, n_lat - 1)), dma((STEPS, n_mem - 1)), dma((STEPS, n_mem - 1)),
        ],
        compiler_params=pltpu.CompilerParams(collective_id=0, has_side_effects=True),
    )(perturbations, ordered, innovations, thresholds, *constants)
    weights, increment = pl.pallas_call(
        copy_kernel, out_shape=shapes, in_specs=[vmem] * 2, out_specs=(whole, whole),
        scratch_shapes=[dma((2,))])(pltpu.with_memory_space_constraint(weights, pltpu.VMEM), pltpu.with_memory_space_constraint(increment, pltpu.VMEM))
    return weights.transpose(1, 0, 2), increment


def solution(mesh):
    return jax.shard_map(
        functools.partial(per_device, mesh.shape["mem"], mesh.shape["lat"]),
        mesh=mesh,
        in_specs=(P("mem", None, "lat", None), P("mem", "lat", None), P(None, "lat", None), P()),
        out_specs=(P("mem", "lat", None), P(None, "lat", "mem")),
        check_vma=False,
    )
```

```python
import functools

import jax
import jax.numpy as jnp
import numpy as np
from jax import lax
from jax.experimental import pallas as pl
from jax.experimental.pallas import tpu as pltpu
from jax.sharding import PartitionSpec as P

RATIO = 4
HALF = 5
STEPS = 2
SIDE = 4
GROUP = 8
PAIR = 2
LANES = 128
MESH = pl.DeviceIdType.MESH
SCALE = 96.0


def tent(distance):
    return np.maximum(0.0, 1.0 - np.abs(distance) / RATIO)


def row_operator(coarse_rows, first, last):
    fine = np.arange(RATIO * coarse_rows)[:, None]
    inner = np.arange(-1, coarse_rows + 1)
    up = tent(fine + 0.5 - RATIO * inner[None, :] - RATIO / 2)
    if first:
        up[:, 0] = 0.0
    if last:
        up[:, -1] = 0.0
    outer = np.arange(-coarse_rows, 2 * coarse_rows)
    gap = np.abs(inner[:, None] - outer[None, :])
    smooth = np.where(gap <= HALF, (1.0 - gap / (HALF + 1)) / 2, 0.0)
    return np.rint(SCALE * up @ smooth)


def block_rows(operator):
    fine, wide = operator.shape
    out = np.zeros((GROUP, fine, wide, GROUP))
    for member in range(GROUP):
        out[member, :, :, member] = operator
    return out.reshape(GROUP * fine, wide * GROUP)


def tables(coarse_rows):
    ops = [block_rows(row_operator(coarse_rows, *ends)) for ends in ((True, False), (False, False), (False, True))]
    rows_up = np.stack(ops)
    rows_down = np.stack([op.T for op in ops])
    fine = np.arange(2 * LANES)[None, :]
    narrow = tent(LANES + fine + 0.5 - RATIO * np.arange(LANES)[:, None] - RATIO / 2)
    wide = tent(3 * LANES + fine + 0.5 - RATIO * np.arange(2 * LANES)[:, None] - RATIO / 2)
    narrow_up = np.concatenate([narrow, narrow], 0)
    wide_up = np.concatenate([wide[:LANES], wide[:LANES], wide[LANES:], wide[LANES:]], 0)
    narrow_down = np.concatenate([narrow.T, narrow.T], 0)
    wide_down = np.concatenate([wide.T, wide.T], 0)
    return [jnp.asarray(t, jnp.bfloat16) for t in (rows_up, rows_down, narrow_up, wide_up, narrow_down, wide_down)]


def split(x):
    high = x.astype(jnp.bfloat16)
    return high, (x - high.astype(jnp.float32)).astype(jnp.bfloat16)


def dot(a, b):
    return jnp.dot(a, b, preferred_element_type=jnp.float32)


def kernel(
    n_mem, n_lat, seg, layout,
    pert_hbm, control_hbm, innov_hbm, thr_hbm, rows_up_hbm, rows_down_hbm, narrow_up_hbm, wide_up_hbm, narrow_down_hbm, wide_down_hbm,
    weights_out, inc_out,
    thr, pert_raw, pert, control, innov, rows_up, rows_down, narrow_up, wide_up, narrow_down, wide_down,
    halo, part_send, part_recv, own, w, spare, lifted, acc, pair_recv, half_sum, z_recv, image, inc, misfit, obs,
    lat_send, lat_recv, mem_send, mem_recv,
    pert_sem, load_sem, g_send, g_recv, c_send, c_recv, p_ss, p_rs, z_ss, z_rs, ag_ss, ag_rs, im_ss, im_rs, sl_ss, sl_rs, sm_ss, sm_rs,
):
    mem = lax.axis_index("mem")
    lat = lax.axis_index("lat")
    core = lax.rem(mem, 2)
    n_z = n_mem // 2
    z = mem // 2
    blocks = pert.shape[0] // GROUP
    chunks = blocks // PAIR
    n_vars = pert.shape[1]
    fine = pert.shape[2]
    tiles = pert.shape[3] // LANES
    pairs = tiles // 2
    tile_rows = n_vars * fine
    half = seg // 2
    n_rows = seg // GROUP
    case = jnp.where(lat == 0, 0, jnp.where(lat == n_lat - 1, 2, 1))
    up_id = (mem, jnp.maximum(lat - 1, 0))
    down_id = (mem, jnp.minimum(lat + 1, n_lat - 1))
    has_up = lat > 0
    has_down = lat < n_lat - 1
    partner = (2 * z + 1 - core, lat)
    z_peers = [(2 * lax.rem(z + k, n_z) + core, lat) for k in range(1, n_z)]
    mem_peers = [(2 * lax.rem(z + k, n_z) + c, lat) for k in (2, 1, 3) for c in (core, 1 - core)] + [partner]
    far = sorted(((i, k) for i in range(SIDE) for k in range(SIDE) if i or k), key=lambda at: -sum(min(d, SIDE - d) for d in at))
    lat_peers = [(mem, lax.rem(lat // SIDE + i, SIDE) * SIDE + lax.rem(lat + k, SIDE)) for i, k in far]
    groups = ((0, seg + half), (seg + half, seg))
    first_rows, tail_rows, second_rows = pl.ds(0, seg), pl.ds(seg, half), pl.ds(seg + half, seg)
    bases, parts, starts = layout
    z_order = sorted(range(n_z - 1), key=lambda k: k + 1 != n_z // 2)
    z_bases = [sum(parts[:i]) for i in range(3)]

    loads = [
        (control_hbm, control), (rows_up_hbm.at[case], rows_up), (narrow_up_hbm, narrow_up), (wide_up_hbm, wide_up),
        (innov_hbm, innov), (rows_down_hbm.at[case], rows_down), (narrow_down_hbm, narrow_down), (wide_down_hbm, wide_down),
        (thr_hbm, thr),
    ]
    loads = [pltpu.make_async_copy(src, dst, load_sem.at[i]) for i, (src, dst) in enumerate(loads)]

    loads[0].start()
    barrier = pltpu.get_barrier_semaphore()
    for peer in lat_peers + mem_peers:
        pl.semaphore_signal(barrier, inc=1, device_id=peer, device_id_type=MESH)

    def pert_copy(c):
        rows = pl.ds(c * GROUP, GROUP)
        return pltpu.make_async_copy(pert_hbm.at[rows], pert_raw.at[rows], pert_sem.at[c])

    for load in loads[1:4]:
        load.start()
    for c in range(blocks):
        pert_copy(c).start()
    for load in loads[4:]:
        load.start()

    lane = lax.broadcasted_iota(jnp.int32, (half, LANES), 1)
    left = lane < LANES // 2

    def swap(x):
        return pltpu.roll(x, LANES // 2, 1)

    def g_copy(q, b, up):
        rows = pl.ds(*groups[q])
        i = 0 if up else 1
        return pltpu.make_async_remote_copy(
            src_ref=halo.at[1, b, rows], dst_ref=halo.at[2 if up else 0, b, rows],
            send_sem=g_send.at[i, q, b], recv_sem=g_recv.at[i, q, b],
            device_id=up_id if up else down_id, device_id_type=MESH)

    def c_copy(q, b, up):
        rows = pl.ds(*groups[q])
        i = 0 if up else 1
        return pltpu.make_async_remote_copy(
            src_ref=part_send.at[i, b, rows], dst_ref=part_recv.at[i, b, rows],
            send_sem=c_send.at[i, q, b], recv_sem=c_recv.at[i, q, b],
            device_id=up_id if up else down_id, device_id_type=MESH)

    def send_both(copy, q, bs):
        @pl.when(has_up)
        def _():
            for b in bs:
                copy(q, b, True).start()

        @pl.when(has_down)
        def _():
            for b in bs:
                copy(q, b, False).start()

    def recv_both(copy, q, bs):
        @pl.when(has_down)
        def _():
            for b in bs:
                copy(q, b, True).wait_recv()

        @pl.when(has_up)
        def _():
            for b in bs:
                copy(q, b, False).wait_recv()

    def sent_all(copy):
        def body(b, carry):
            for q in range(2):
                @pl.when(has_up)
                def _():
                    copy(q, b, True).wait_send()

                @pl.when(has_down)
                def _():
                    copy(q, b, False).wait_send()
            return carry

        lax.fori_loop(0, blocks, body, 0)

    def over_chunks(f):
        def body(c, carry):
            f([c * PAIR + i for i in range(PAIR)])
            return carry

        lax.fori_loop(0, chunks, body, 0)

    def lane_pair(j):
        return 2 * j + 1, (2 * j + 2) % tiles

    def flat_rows(j, v):
        return pl.ds(starts[j] + v * fine, fine)

    def both_pieces(x):
        high, low = split(x)
        return jnp.concatenate([high, low], axis=1)

    def lift(g, b):
        pieces = []
        for i in range(3):
            if g < 2:
                pieces.append(halo[i, b, second_rows if g else first_rows, :])
            else:
                first = halo[i, b, first_rows, :]
                tail = halo[i, b, tail_rows, :]
                pieces.append(jnp.where(left, tail, swap(first[:half])))
                pieces.append(jnp.where(left, swap(tail), swap(first[half:])))
        wide = dot(rows_up[...], both_pieces(jnp.concatenate(pieces, axis=0)))
        return both_pieces(wide[:, :LANES] + wide[:, LANES:])

    def accumulate(j, bs, fields):
        for h, t in enumerate(lane_pair(j)):
            for v in range(n_vars):
                total = acc[h, flat_rows(j, v), :]
                for b, field in zip(bs, fields):
                    f = field[:, h * LANES:(h + 1) * LANES].reshape(GROUP, fine, LANES)
                    p = pert[pl.ds(b * GROUP, GROUP), v, :, t * LANES:(t + 1) * LANES]
                    total = total + jnp.sum(p * f, axis=0)
                acc[h, flat_rows(j, v), :] = total

    def forward_first(bs):
        recv_both(g_copy, 0, bs)
        zero_th = [lift(0, b) for b in bs]
        two = [lift(2, b) for b in bs]
        for b, p, q in zip(bs, zero_th, two):
            lifted[b, 0] = p
            lifted[b, 1] = q
        accumulate(0, bs, [dot(value, narrow_up[...]) for value in zero_th])
        accumulate(4, bs, [dot(value, narrow_up[...]) for value in two])

    def odd_tile(a, b):
        return dot(a, wide_up[:2 * LANES, :]) + dot(b, wide_up[2 * LANES:, :])

    def forward_second(b, split_at=None):
        recv_both(g_copy, 1, [b])
        one = lift(1, b)
        accumulate(1, [b], [odd_tile(lifted[b, 0], one)])
        accumulate(2, [b], [dot(one, narrow_up[...])])
        if split_at is not None:
            split_at()
        accumulate(3, [b], [odd_tile(one, lifted[b, 1])])

    def weighted(j, b):
        pieces = []
        for h, t in enumerate(lane_pair(j)):
            total = None
            for v in range(n_vars):
                p = pert[pl.ds(b * GROUP, GROUP), v, :, t * LANES:(t + 1) * LANES]
                term = p * misfit[h, flat_rows(j, v), :][None]
                total = term if total is None else total + term
            pieces.append(split(total.reshape(GROUP * fine, LANES)))
        lhs = jnp.concatenate([pieces[0][0], pieces[1][0], pieces[0][1], pieces[1][1]], axis=1)
        return dot(lhs, narrow_down[...] if j % 2 == 0 else wide_down[...])

    def lower(x):
        wide = dot(rows_down[...], both_pieces(x))
        return (wide[:, :LANES] + wide[:, LANES:]) * (1.0 / SCALE)

    def keep(b, rows, coarse):
        part_send[0, b, rows, :] = coarse[0]
        own[b, rows, :] = coarse[1]
        part_send[1, b, rows, :] = coarse[2]

    def three(x):
        return x[:seg], x[seg:2 * seg], x[2 * seg:]

    def adjoint_first(bs):
        for b in bs:
            last = weighted(4, b)
            wide = weighted(1, b)
            high = weighted(3, b)
            wrapped = jnp.where(lax.broadcasted_iota(jnp.int32, last.shape, 1) < LANES // 2, swap(last), 0.0)
            first = weighted(0, b) + wide[:, :LANES] + wrapped
            spare[b] = wide[:, LANES:] + high[:, :LANES]
            keep(b, first_rows, three(lower(first)))
            ends = three(lower(last + high[:, LANES:]))
            keep(b, tail_rows, [jnp.where(left, e[:half], swap(e[half:])) for e in ends])
        send_both(c_copy, 0, bs)

    def adjoint_second(bs):
        for b in bs:
            keep(b, second_rows, three(lower(spare[b] + weighted(2, b))))
        send_both(c_copy, 1, bs)

    def region(s):
        return pl.ds(bases[s], n_z * parts[s])

    def part_rows(s, at):
        return pl.ds(pl.multiple_of(bases[s] + at * parts[s], 8), parts[s])

    def pair_copy(s):
        return pltpu.make_async_remote_copy(
            src_ref=acc.at[1 - core, region(s)], dst_ref=pair_recv.at[region(s)],
            send_sem=p_ss.at[s], recv_sem=p_rs.at[s], device_id=partner, device_id_type=MESH)

    def z_copy(s, k):
        return pltpu.make_async_remote_copy(
            src_ref=half_sum.at[part_rows(s, lax.rem(z + k + 1, n_z))], dst_ref=z_recv.at[k, pl.ds(z_bases[s], parts[s])],
            send_sem=z_ss.at[s, k], recv_sem=z_rs.at[s, k], device_id=z_peers[k], device_id_type=MESH)

    def ag_copy(s, k, source):
        return pltpu.make_async_remote_copy(
            src_ref=image.at[core, part_rows(s, source)], dst_ref=image.at[core, part_rows(s, source)],
            send_sem=ag_ss.at[s, k], recv_sem=ag_rs.at[s, k], device_id=z_peers[k], device_id_type=MESH)

    def image_copy(index):
        return pltpu.make_async_remote_copy(
            src_ref=image.at[index], dst_ref=image.at[index],
            send_sem=im_ss.at[0], recv_sem=im_rs.at[0], device_id=partner, device_id_type=MESH)

    def pair_finish(s):
        pair_copy(s).wait_recv()
        half_sum[region(s), :] = acc[core, region(s), :] + pair_recv[region(s), :]
        for k in z_order:
            z_copy(s, k).start()

    def z_finish(s, early):
        for k in range(n_z - 1):
            z_copy(s, k).wait_recv()
        total = half_sum[part_rows(s, z), :]
        for k in range(n_z - 1):
            total = total + z_recv[k, pl.ds(z_bases[s], parts[s]), :]
        total = total * (1.0 / SCALE)
        image[core, part_rows(s, z), :] = total
        if s < early:
            gather_start(s)
        return total_of(total * total)

    def gather_start(s):
        for k in z_order:
            ag_copy(s, k, z).start()

    def gather_pass():
        for s in range(3):
            for k in range(n_z - 1):
                ag_copy(s, k, lax.rem(z + n_z - 1 - k, n_z)).wait_recv()
        image_copy(core).start()

    def gather_finish():
        image_copy(1 - core).wait_recv()
        image_copy(core).wait_send()
        for s in range(3):
            pair_copy(s).wait_send()
            for k in range(n_z - 1):
                z_copy(s, k).wait_send()
                ag_copy(s, k, z).wait_send()

    def total_of(squares):
        return jnp.sum(squares.reshape(-1, 8, LANES), axis=0)

    def forward_all(early):
        acc[...] = jnp.zeros_like(acc)
        over_chunks(forward_first)
        pair_copy(0).start()

        def body(b, carry):
            forward_second(b)
            return carry

        lax.fori_loop(0, blocks - 1, body, 0)
        pair_finish(0)
        forward_second(blocks - 1, lambda: pair_copy(1).start())
        pair_copy(2).start()
        pair_finish(1)
        pair_finish(2)
        squares = z_finish(0, early)
        squares = squares + z_finish(1, early)
        squares = squares + z_finish(2, early)
        return squares

    def sl_copy(it, k):
        return pltpu.make_async_remote_copy(
            src_ref=lat_send, dst_ref=lat_recv.at[it, k],
            send_sem=sl_ss.at[it, k], recv_sem=sl_rs.at[it, k], device_id=lat_peers[k], device_id_type=MESH)

    def sm_copy(it, k):
        return pltpu.make_async_remote_copy(
            src_ref=mem_send, dst_ref=mem_recv.at[it, k],
            send_sem=sm_ss.at[it, k], recv_sem=sm_rs.at[it, k], device_id=mem_peers[k], device_id_type=MESH)

    loads[0].wait()
    for b in range(blocks):
        block = control[:, pl.ds(b * GROUP, GROUP), :].reshape(seg, control.shape[2])
        ends = block[:, 2 * LANES:]
        tail = jnp.concatenate([ends[:half], ends[half:]], axis=1)
        for rows, value in ((first_rows, block[:, :LANES]), (second_rows, block[:, LANES:2 * LANES]), (tail_rows, tail)):
            halo[1, b, rows, :] = value
            w[b, rows, :] = value

    pl.semaphore_wait(barrier, len(lat_peers) + len(mem_peers))
    over_chunks(functools.partial(send_both, g_copy, 0))
    over_chunks(functools.partial(send_both, g_copy, 1))

    zero = jnp.zeros(halo.shape[2:], jnp.float32)

    @pl.when(jnp.logical_not(has_up))
    def _():
        for b in range(blocks):
            halo[0, b] = zero
            part_recv[1, b] = zero

    @pl.when(jnp.logical_not(has_down))
    def _():
        for b in range(blocks):
            halo[2, b] = zero
            part_recv[0, b] = zero

    for load in loads[1:]:
        load.wait()
    for j in range(pairs):
        for h, t in enumerate(lane_pair(j)):
            for v in range(n_vars):
                obs[h, flat_rows(j, v), :] = innov[v, :, t * LANES:(t + 1) * LANES]
    for c in range(blocks):
        pert_copy(c).wait()

    def widen(m, carry):
        pert[m] = pert_raw[m].astype(jnp.float32)
        return carry

    lax.fori_loop(0, pert.shape[0], widen, 0)
    forward_all(2)
    gather_start(2)
    sent_all(g_copy)
    gather_pass()
    gather_finish()
    inc[...] = image[...]

    def step(it, step_len):
        for h in range(2):
            for j in (4, 0, 1, 3, 2):
                for v in range(n_vars):
                    rows = flat_rows(j, v)
                    moved = inc[h, rows, :] - step_len * image[h, rows, :]
                    inc[h, rows, :] = moved
                    misfit[h, rows, :] = jnp.clip(moved - obs[h, rows, :], -thr[v], thr[v])
        for bs in ((0,), (1,), (2,), (3,)):
            adjoint_first(bs)
        over_chunks(adjoint_second)
        for b in range(blocks):
            w[b] = w[b] - step_len * halo[1, b]

        def gradient(q):
            def body(b, squares):
                recv_both(c_copy, q, [b])
                rows = pl.ds(*groups[q])
                grad = w[b, rows, :] + own[b, rows, :] + part_recv[0, b, rows, :] + part_recv[1, b, rows, :]
                halo[1, b, rows, :] = grad
                send_both(g_copy, q, [b])
                return squares + total_of(grad * grad)

            return lax.fori_loop(0, blocks, body, jnp.zeros((8, LANES), jnp.float32))

        grad_sq = gradient(0)
        grad_sq = grad_sq + gradient(1)
        image_sq = forward_all(1)
        sums = jnp.concatenate([jnp.sum(grad_sq, axis=0, keepdims=True), jnp.sum(image_sq, axis=0, keepdims=True)], axis=0)
        mem_send[...] = sums
        for k in range(n_mem - 1):
            sm_copy(it, k).start()
        gather_start(1)
        gather_start(2)
        sent_all(c_copy)
        sent_all(g_copy)
        for k in range(n_mem - 1):
            sm_copy(it, k).wait_recv()
        sums = sums + jnp.sum(mem_recv[it], axis=0)
        lat_send[...] = sums
        for k in range(n_lat - 1):
            sl_copy(it, k).start()
        gather_pass()
        gather_finish()
        for k in range(n_lat - 1):
            sl_copy(it, k).wait_recv()
        sums = sums + jnp.sum(lat_recv[it], axis=0)
        for k in range(n_lat - 1):
            sl_copy(it, k).wait_send()
        g2 = jnp.sum(sums[0:1, :], axis=1, keepdims=True)
        h2 = jnp.sum(sums[1:2, :], axis=1, keepdims=True)
        step_len = g2 / (g2 + h2)
        for k in range(n_mem - 1):
            sm_copy(it, k).wait_send()
        return step_len

    step_len = lax.fori_loop(0, STEPS, step, jnp.zeros((1, 1), jnp.float32))

    for b in range(blocks):
        members = pl.ds(b * GROUP, GROUP)
        final = w[b] - step_len * halo[1, b]
        one, tail, two = final[:seg], final[seg:seg + half], final[seg + half:]
        weights_out[:, members, :LANES] = one.reshape(n_rows, GROUP, LANES)
        weights_out[:, members, LANES:2 * LANES] = two.reshape(n_rows, GROUP, LANES)
        weights_out[:n_rows // 2, members, 2 * LANES:] = tail[:, :LANES // 2].reshape(n_rows // 2, GROUP, LANES // 2)
        weights_out[n_rows // 2:, members, 2 * LANES:] = tail[:, LANES // 2:].reshape(n_rows // 2, GROUP, LANES // 2)

    share = inc_out.shape[2]
    first = mem * share // LANES
    shift = mem * share - first * LANES

    def lane_tile(t, v):
        j = jnp.where(t % 2 == 1, (t - 1) // 2, (t // 2 + pairs - 1) % pairs)
        row = jnp.int32(0)
        for i in range(pairs):
            row = jnp.where(j == i, starts[i] + v * fine, row)
        rows = pl.ds(pl.multiple_of(row, 8), fine)
        return inc[1 - t % 2, rows, :] - step_len * image[1 - t % 2, rows, :]

    fine_lane = lax.broadcasted_iota(jnp.int32, (fine, LANES), 1)
    for v in range(n_vars):
        a = pltpu.roll(lane_tile(first, v), (LANES - shift) % LANES, 1)
        b = pltpu.roll(lane_tile(first + 1, v), (LANES - shift) % LANES, 1)
        inc_out[v, :, :LANES] = jnp.where(fine_lane < LANES - shift, a, b)
        inc_out[v, :, LANES:] = b[:, :share - LANES]


def copy_kernel(a_ref, b_ref, c_ref, d_ref, sems):
    copies = [pltpu.make_async_copy(a_ref, c_ref, sems.at[0]), pltpu.make_async_copy(b_ref, d_ref, sems.at[1])]
    for copy in copies:
        copy.start()
    for copy in copies:
        copy.wait()


def per_device(n_mem, n_lat, perturbations, control, innovations, thresholds):
    members, coarse_rows, coarse_cols = control.shape
    n_vars, fine_rows, fine_cols = innovations.shape
    blocks = members // GROUP
    seg = GROUP * coarse_rows
    packed = seg * coarse_cols // LANES
    n_z = n_mem // 2
    tile_rows = n_vars * fine_rows
    pairs = fine_cols // (2 * LANES)
    parts, bases, flat = [], [], 0
    starts = [0] * pairs
    for tiles in ((0, 4), (1, 2), (3,)):
        parts.append(-(-len(tiles) * tile_rows // n_z // 8) * 8)
        bases.append(flat)
        for i, j in enumerate(tiles):
            starts[j] = flat + i * tile_rows
        flat += n_z * parts[-1]
    vmem = pl.BlockSpec(memory_space=pltpu.VMEM)
    whole = pl.BlockSpec(memory_space=pl.ANY)
    f32 = jnp.float32
    bf16 = jnp.bfloat16
    dma = pltpu.SemaphoreType.DMA
    constants = tables(coarse_rows)
    ordered = control.transpose(1, 0, 2)
    shapes = (
        jax.ShapeDtypeStruct(ordered.shape, f32),
        jax.ShapeDtypeStruct((n_vars, fine_rows, fine_cols // n_mem), f32))
    weights, increment = pl.pallas_call(
        functools.partial(kernel, n_mem, n_lat, seg, (bases, parts, starts)),
        out_shape=tuple(pltpu.VMEM(x.shape, f32) for x in shapes),
        in_specs=[whole] * 10,
        out_specs=(vmem, vmem),
        scratch_shapes=[
            pltpu.SMEM(thresholds.shape, f32),
            pltpu.VMEM(perturbations.shape, bf16),
            pltpu.VMEM(perturbations.shape, f32),
            pltpu.VMEM(ordered.shape, f32),
            pltpu.VMEM(innovations.shape, f32),
            pltpu.VMEM(constants[0].shape[1:], bf16),
            pltpu.VMEM(constants[1].shape[1:], bf16),
            pltpu.VMEM(constants[2].shape, bf16),
            pltpu.VMEM(constants[3].shape, bf16),
            pltpu.VMEM(constants[4].shape, bf16),
            pltpu.VMEM(constants[5].shape, bf16),
            pltpu.VMEM((3, blocks, packed, LANES), f32),
            pltpu.VMEM((2, blocks, packed, LANES), f32),
            pltpu.VMEM((2, blocks, packed, LANES), f32),
            pltpu.VMEM((blocks, packed, LANES), f32),
            pltpu.VMEM((blocks, packed, LANES), f32),
            pltpu.VMEM((blocks, GROUP * fine_rows, LANES), f32),
            pltpu.VMEM((blocks, 2, GROUP * fine_rows, 2 * LANES), bf16),
            pltpu.VMEM((2, flat, LANES), f32),
            pltpu.VMEM((flat, LANES), f32),
            pltpu.VMEM((flat, LANES), f32),
            pltpu.VMEM((n_z - 1, sum(parts), LANES), f32),
            pltpu.VMEM((2, flat, LANES), f32),
            pltpu.VMEM((2, flat, LANES), f32),
            pltpu.VMEM((2, flat, LANES), f32),
            pltpu.VMEM((2, flat, LANES), f32),
            pltpu.VMEM((2, LANES), f32),
            pltpu.VMEM((STEPS, n_lat - 1, 2, LANES), f32),
            pltpu.VMEM((2, LANES), f32),
            pltpu.VMEM((STEPS, n_mem - 1, 2, LANES), f32),
            dma((blocks,)), dma((9,)),
            dma((2, 2, blocks)), dma((2, 2, blocks)), dma((2, 2, blocks)), dma((2, 2, blocks)),
            dma((3,)), dma((3,)), dma((3, n_z - 1)), dma((3, n_z - 1)), dma((3, n_z - 1)), dma((3, n_z - 1)), dma((1,)), dma((1,)),
            dma((STEPS, n_lat - 1)), dma((STEPS, n_lat - 1)), dma((STEPS, n_mem - 1)), dma((STEPS, n_mem - 1)),
        ],
        compiler_params=pltpu.CompilerParams(collective_id=0, has_side_effects=True),
    )(perturbations, ordered, innovations, thresholds, *constants)
    weights, increment = pl.pallas_call(
        copy_kernel, out_shape=shapes, in_specs=[vmem] * 2, out_specs=(whole, whole),
        scratch_shapes=[dma((2,))])(pltpu.with_memory_space_constraint(weights, pltpu.VMEM), pltpu.with_memory_space_constraint(increment, pltpu.VMEM))
    return weights.transpose(1, 0, 2), increment


def solution(mesh):
    return jax.shard_map(
        functools.partial(per_device, mesh.shape["mem"], mesh.shape["lat"]),
        mesh=mesh,
        in_specs=(P("mem", None, "lat", None), P("mem", "lat", None), P(None, "lat", None), P()),
        out_specs=(P("mem", "lat", None), P(None, "lat", "mem")),
        check_vma=False,
    )
```
